256 devices in a mesh: fsdp: 16 (over y_lo, x, core), ctx: 16 (over y_hi, z).
Axes of the slice: x: 4, y: 4 (y_hi: 2, y_lo: 2; y = y_hi * 2 + y_lo), z: 8, core: 2. Of those that a mesh axis runs over, the one named last changes fastest.
Arguments:
- q_raw: bfloat16 [16, 4096, 1536], P('fsdp', 'ctx')
- k_raw: bfloat16 [16, 4096, 1536], P('fsdp', 'ctx')
- values_in: bfloat16 [16, 4096, 1536], P('fsdp', 'ctx'), may hold values from -6 to 6
- d_out: bfloat16 [16, 4096, 1536], P('fsdp', 'ctx'), may hold values from -6 to 6
- gains: float32 [2, 128], P(None, 'fsdp')
- tile_device: int32 [16], replicated, may hold values from 0 to 15, as said below
- neighbours: int32 [16, 6], replicated, may hold values from -1 to 15, as said below
Outputs:
- attended: bfloat16 [16, 4096, 1536], P('fsdp', 'ctx')
- dq_raw: bfloat16 [16, 4096, 1536], P('fsdp', 'ctx')
- dk_raw: bfloat16 [16, 4096, 1536], P('fsdp', 'ctx')
- value_grad: bfloat16 [16, 4096, 1536], P('fsdp', 'ctx')
The draws below stay inside these ranges and needn't reach their ends.
Inputs may be any that keep to these rules, and one draw needn't show every extreme that they name: `tile_device`: the entries are a permutation of the ctx indices, and tile t lies on device 2 (t // 2) or 2 (t // 2) + 1, so the two tiles of a grid column sit on one pair of devices and columns follow in order. `neighbours`: row t holds t in slot 0; slots 1 to 5 hold, in an order that differs from row to row, the other tile of t's column and some of the tiles of the adjacent columns, -1 in the other slots.
All inputs are finite; a program needn't handle non-finite values.
Results may differ from the reference program's by a relative error of at most 0.028.
The reference program's roundings to bfloat16 on the way count: a program that leaves them out, or rounds other values in their place, can miss the bound.
Values may be sent and summed in bfloat16 or wider, within the bound.
No kernel may reach another device: no remote copies, remote signals or barrier semaphores. Data moves between devices by JAX's collectives and lax.ppermute only.
A program may use at most 192 MiB of HBM per device.

```python
import math
import jax
import jax.numpy as jnp
from jax import lax

HEADS = 12
HD = 128
TILE = 256
F = 1536
TILES = 16
GW = 8
TOKENS = 4096
CLIPS = 16


def query_key(key):
    base_query = jax.random.normal(jax.random.fold_in(key, 101), (CLIPS, TOKENS, F), jnp.float32)
    base_key = jax.random.normal(jax.random.fold_in(key, 102), (CLIPS, TOKENS, F), jnp.float32)
    return (jnp.clip(base_query, -6.0, 6.0), jnp.clip(base_key, -6.0, 6.0))


def draw_q_raw(key, part):
    return query_key(key)[0].astype(jnp.bfloat16)


def draw_k_raw(key, part):
    return query_key(key)[1].astype(jnp.bfloat16)


def draw_gains(key, part):
    return jnp.exp(jax.random.uniform(key, (2, HD), jnp.float32, math.log(0.5), math.log(2.0)))


def draw_tile_device(key, part):
    tile_ids = jnp.arange(TILES, dtype=jnp.int32)
    flip_bits = jax.random.randint(key, (GW,), 0, 2, dtype=jnp.int32)
    column = tile_ids // 2
    flip_tile = jnp.sum(jnp.where(column[:, None] == jnp.arange(GW, dtype=jnp.int32)[None, :], flip_bits[None, :], 0), axis=1)
    return (2 * column + (tile_ids % 2 + flip_tile) % 2).astype(jnp.int32)


def draw_neighbours(key, part):
    tile_ids = jnp.arange(TILES, dtype=jnp.int32)
    column = tile_ids // 2
    row_bit = tile_ids % 2
    candidates = jnp.stack([2 * column + 1 - row_bit, 2 * column - 2, 2 * column - 1, 2 * column + 2, 2 * column + 3], axis=1)
    keep_bits = jax.random.randint(jax.random.fold_in(key, 9), (TILES, 4), 0, 2, dtype=jnp.int32)
    always = column >= 0
    before = column >= 1
    after = column + 1 < GW
    valid = jnp.stack([always, jnp.logical_and(before, keep_bits[:, 0] == 1), jnp.logical_and(before, keep_bits[:, 1] == 1), jnp.logical_and(after, keep_bits[:, 2] == 1), jnp.logical_and(after, keep_bits[:, 3] == 1)], axis=1)
    slots = jnp.where(valid, candidates, -1)
    priority = jax.random.randint(jax.random.fold_in(key, 7), (TILES, 5), 0, 1000, dtype=jnp.int32) * 8 + jnp.arange(5, dtype=jnp.int32)[None, :]
    order = jnp.argsort(priority, axis=1, stable=True)
    shuffled = jnp.take_along_axis(slots, order, axis=1)
    return jnp.concatenate([tile_ids[:, None], shuffled], axis=1).astype(jnp.int32)


def block_scale(stream_key, shape, cuts, least, high):
    def one(dim, parts):
        draws = jax.random.uniform(jax.random.fold_in(jax.random.fold_in(stream_key, 6), dim), (parts,), jnp.float32, least / len(cuts), high / len(cuts))
        return jnp.repeat(jnp.exp(draws), shape[dim] // parts).reshape((-1,) + (1,) * (len(shape) - dim - 1))

    gain = one(*cuts[0])
    for cut in cuts[1:]:
        gain = gain * one(*cut)
    return gain


def bell_draw(own_key, dims, width, bound, split=(), kind=jnp.bfloat16):
    array = width * jax.random.normal(own_key, dims, jnp.float32)
    if split:
        array = array * block_scale(own_key, dims, split, -0.22, 0.18)
    return jnp.clip(array, -bound, bound).astype(kind)


def setup_inputs(seed: int = 0) -> dict:
    key_list = jax.random.split(jax.random.key(seed), 8)
    return {
        "q_raw": draw_q_raw(jax.random.fold_in(key_list[7], 71), 0),
        "k_raw": draw_k_raw(jax.random.fold_in(key_list[7], 71), 0),
        "values_in": bell_draw(key_list[2], (CLIPS, TOKENS, F), 1.0, 6.0, ((0, 16), (1, 16))),
        "d_out": bell_draw(key_list[3], (CLIPS, TOKENS, F), 1.0, 6.0, ((0, 16), (1, 16))),
        "gains": draw_gains(jax.random.fold_in(key_list[7], 71), 0),
        "tile_device": draw_tile_device(jax.random.fold_in(key_list[7], 71), 0),
        "neighbours": draw_neighbours(jax.random.fold_in(key_list[7], 71), 0),
    }


EPSILON = 1e-06

def narrow(values):
    return lax.optimization_barrier(values.astype(jnp.bfloat16))

def normalize(raw_rows, gain_row):
    floats = raw_rows.astype(jnp.float32).reshape(raw_rows.shape[0], HEADS, HD)
    inverse = lax.rsqrt(lax.optimization_barrier(jnp.mean(floats * floats, axis=-1, keepdims=True)) + EPSILON)
    return (floats, inverse, narrow(floats * inverse * gain_row))

def denormalize(floats, inverse, gain_row, upstream):
    scaled = upstream * gain_row
    inner_sum = lax.optimization_barrier(jnp.mean(floats * scaled, axis=-1, keepdims=True))
    result = inverse * scaled - floats * inverse * inverse * inverse * inner_sum
    return result.reshape(floats.shape[0], HEADS * HD).astype(jnp.bfloat16)

def reference(q_raw, k_raw, values_in, d_out, gains, tile_device, neighbours):
    score_scale = HD ** (-0.5)
    tile_ids = jnp.arange(TILES, dtype=jnp.int32)
    block_tile = lax.optimization_barrier(jnp.sum(jnp.where(tile_device[None, :] == tile_ids[:, None], tile_ids[None, :], 0), axis=1)).astype(jnp.int32)

    def one_clip(clip_index):
        q_float, q_inv, q_normed = normalize(q_raw[clip_index], gains[0])
        k_float, k_inv, k_normed = normalize(k_raw[clip_index], gains[1])
        query_blocks = q_normed.reshape(TILES, TILE, HEADS, HD)
        key_blocks = k_normed.reshape(TILES, TILE, HEADS, HD)
        value_blocks = values_in[clip_index].reshape(TILES, TILE, HEADS, HD)
        grad_blocks = d_out[clip_index].reshape(TILES, TILE, HEADS, HD)

        def one_block(block_index):
            slots = neighbours[block_tile[block_index]]
            valid = slots >= 0
            key_index = tile_device[jnp.maximum(slots, 0)].astype(jnp.int32)
            key_rows = key_blocks[key_index].astype(jnp.float32)
            value_rows = value_blocks[key_index].astype(jnp.float32)
            query_rows = query_blocks[block_index].astype(jnp.float32)
            grad_rows = grad_blocks[block_index].astype(jnp.float32)
            logits = jnp.einsum('qhd,nkhd->hqnk', query_rows, key_rows) * score_scale
            logits = jnp.where(valid[None, None, :, None], logits, -jnp.inf)
            row_max = lax.optimization_barrier(jnp.max(logits, axis=(2, 3)))
            row_total = lax.optimization_barrier(jnp.sum(jnp.exp(logits - row_max[:, :, None, None]), axis=(2, 3)))
            lse = row_max + jnp.log(row_total)
            probs = jnp.exp(logits - lse[:, :, None, None])
            probs_low = narrow(probs).astype(jnp.float32)
            attended = narrow(jnp.einsum('hqnk,nkhd->qhd', probs_low, value_rows))
            delta = lax.optimization_barrier(jnp.sum(grad_rows * attended.astype(jnp.float32), axis=-1))
            dprobs = jnp.einsum('qhd,nkhd->hqnk', grad_rows, value_rows)
            dscores = narrow(probs * (dprobs - delta.T[:, :, None, None])).astype(jnp.float32)
            dq_part = jnp.einsum('hqnk,nkhd->qhd', dscores, key_rows) * score_scale
            dk_part = jnp.einsum('hqnk,qhd->nkhd', dscores, query_rows) * score_scale
            dv_part = jnp.einsum('hqnk,qhd->nkhd', probs_low, grad_rows)
            dk_part = jnp.where(valid[:, None, None, None], narrow(dk_part).astype(jnp.float32), 0.0)
            dv_part = jnp.where(valid[:, None, None, None], narrow(dv_part).astype(jnp.float32), 0.0)
            return (attended, dq_part, dk_part, dv_part, key_index)
        attended, dq_part, dk_part, dv_part, key_index = lax.map(one_block, tile_ids)
        flat_index = key_index.reshape(-1)
        dk_sum = jnp.zeros((TILES, TILE, HEADS, HD), jnp.float32).at[flat_index].add(dk_part.reshape(-1, TILE, HEADS, HD))
        dv_sum = jnp.zeros((TILES, TILE, HEADS, HD), jnp.float32).at[flat_index].add(dv_part.reshape(-1, TILE, HEADS, HD))
        dq_out = denormalize(q_float, q_inv, gains[0], dq_part.reshape(TOKENS, HEADS, HD))
        dk_out = denormalize(k_float, k_inv, gains[1], dk_sum.reshape(TOKENS, HEADS, HD))
        return (attended.reshape(TOKENS, F).astype(jnp.bfloat16), dq_out, dk_out, dv_sum.reshape(TOKENS, F).astype(jnp.bfloat16))
    result = lax.map(one_clip, jnp.arange(CLIPS, dtype=jnp.int32))
    return (result[0], result[1], result[2], result[3])
```

```python
import math
from functools import partial

import jax
import jax.numpy as jnp
from jax import lax
from jax.experimental import pallas as pl
from jax.experimental.pallas import tpu as pltpu
from jax.sharding import PartitionSpec as P

EPSILON = 1e-06
ROWS = 256
HD = 128
HB = 2
LOW = -1e30
BF = jnp.bfloat16
F32 = jnp.float32

NT = (((1,), (1,)), ((), ()))
TN = (((0,), (0,)), ((), ()))
NN = (((1,), (0,)), ((), ()))


def dot(a, b, dims):
    return lax.dot_general(a, b, dims, preferred_element_type=F32)


def allowed(sc, query_dev, key_dev):
    count = sc[1]
    inside = jnp.logical_and(
        jnp.logical_and(query_dev >= 0, query_dev < count),
        jnp.logical_and(key_dev >= 0, key_dev < count),
    )

    def tile_at(dev):
        first = 2 * (jnp.clip(dev, 0, count - 1) // 2)
        return jnp.where(sc[2 + first] == dev, first, first + 1)

    query_tile, key_tile = tile_at(query_dev), tile_at(key_dev)
    base = 2 + count + query_tile * 6
    hit = sc[base] == key_tile
    for slot in range(1, 6):
        hit = jnp.logical_or(hit, sc[base + slot] == key_tile)
    return jnp.logical_and(inside, hit)


def around(sc):
    me = sc[0]
    odd = me % 2 == 1
    partner = jnp.where(odd, me - 1, me + 1)
    near = jnp.where(odd, me + 1, me - 1)
    far = jnp.where(odd, me + 2, me - 2)
    return me, partner, near, far


def normed(raw, gain_row):
    floats = raw.astype(F32)
    inverse = lax.rsqrt(jnp.mean(floats * floats, axis=1, keepdims=True) + EPSILON)
    return (floats * inverse * gain_row).astype(BF)


def denormed(raw, gain_row, upstream):
    floats = raw.astype(F32)
    inverse = lax.rsqrt(jnp.mean(floats * floats, axis=1, keepdims=True) + EPSILON)
    scaled = upstream * gain_row
    inner = jnp.mean(floats * scaled, axis=1, keepdims=True)
    return (inverse * scaled - floats * (inverse * inverse * inverse * inner)).astype(BF)


def cols(j):
    return slice(j * HD, (j + 1) * HD)


def forward_unit(kn, v, qn, m_ref, l_ref, acc_ref, j, first=False):
    s = dot(kn, qn, NT) * (math.log2(math.e) / math.sqrt(HD))
    top = jnp.max(s, axis=0, keepdims=True)
    if first:
        p = jnp.exp2(s - top)
        m_ref[j] = top
        l_ref[j] = jnp.sum(p, axis=0, keepdims=True)
        acc_ref[cols(j), :] = dot(v, p.astype(BF), TN)
        return
    old = m_ref[j]
    new = jnp.maximum(old, top)
    shrink = jnp.exp2(old - new)
    p = jnp.exp2(s - new)
    m_ref[j] = new
    l_ref[j] = l_ref[j] * shrink + jnp.sum(p, axis=0, keepdims=True)
    acc_ref[cols(j), :] = acc_ref[cols(j), :] * shrink + dot(v, p.astype(BF), TN)


def backward_unit(kn, v, qn, d_out, lse, delta):
    s = dot(kn, qn, NT) * (math.log2(math.e) / math.sqrt(HD))
    p = jnp.exp2(s - lse)
    dp = dot(v, d_out, NT)
    return p, (p * (dp - delta)).astype(BF)


def row(ref, index):
    return ref[pl.ds(index, 1), :]


def partner_forward(sc, g, q, ke, ve, kf, vf, o_ref, ml_ref, kne, knf, qn, m_ref, l_ref, acc_ref):
    step = pl.program_id(0)
    heads = pl.num_programs(0) * HB
    me, partner, near, far = around(sc)
    for j in range(HB):
        qn[:, cols(j)] = normed(q[:, cols(j)], g[0:1, :])
        kne[:, cols(j)] = normed(ke[:, cols(j)], g[1:2, :])
        knf[:, cols(j)] = normed(kf[:, cols(j)], g[1:2, :])
    m_ref[...] = jnp.full_like(m_ref, LOW)
    l_ref[...] = jnp.zeros_like(l_ref)
    acc_ref[...] = jnp.zeros_like(acc_ref)
    for key_dev, kn, v in ((near, kne, ve), (far, knf, vf)):
        @pl.when(allowed(sc, partner, key_dev))
        def _():
            for j in range(HB):
                forward_unit(
                    kn[:, cols(j)], v[:, cols(j)], qn[:, cols(j)], m_ref, l_ref, acc_ref, j
                )
    for j in range(HB):
        total = l_ref[j]
        ml_ref[pl.ds(step * HB + j, 1), :] = m_ref[j]
        ml_ref[pl.ds(heads + step * HB + j, 1), :] = total
        share = jnp.where(total > 0.0, 1.0 / jnp.where(total > 0.0, total, 1.0), 0.0)
        o_ref[cols(j), :] = (acc_ref[cols(j), :] * share).astype(BF)


def own_forward(
    sc, g, q, k, v, kp, vp, kne, ve, knf, vf, acc_ref, ml_ref, qn, knx, knp, m_ref, l_ref
):
    step = pl.program_id(0)
    heads = pl.num_programs(0) * HB
    me, partner, near, far = around(sc)
    for j in range(HB):
        qn[:, cols(j)] = normed(q[:, cols(j)], g[0:1, :])
        knx[:, cols(j)] = normed(k[:, cols(j)], g[1:2, :])
        knp[:, cols(j)] = normed(kp[:, cols(j)], g[1:2, :])
    for j in range(HB):
        forward_unit(
            knx[:, cols(j)], v[:, cols(j)], qn[:, cols(j)], m_ref, l_ref, acc_ref, j, first=True
        )
    for key_dev, kn, val in ((partner, knp, vp), (near, kne, ve), (far, knf, vf)):
        @pl.when(allowed(sc, me, key_dev))
        def _():
            for j in range(HB):
                forward_unit(
                    kn[:, cols(j)], val[:, cols(j)], qn[:, cols(j)], m_ref, l_ref, acc_ref, j
                )
    for j in range(HB):
        ml_ref[pl.ds(step * HB + j, 1), :] = m_ref[j]
        ml_ref[pl.ds(heads + step * HB + j, 1), :] = l_ref[j]


def merge(acc_ref, ml_ref, o_ret, ml_ret, d_out, att_ref, st_ref):
    step = pl.program_id(0)
    heads = pl.num_programs(0) * HB
    for j in range(HB):
        h = step * HB + j
        m1, l1 = row(ml_ref, h), row(ml_ref, heads + h)
        m2, l2 = row(ml_ret, h), row(ml_ret, heads + h)
        m = jnp.maximum(m1, m2)
        a1 = jnp.exp2(m1 - m)
        a2 = jnp.exp2(m2 - m) * l2
        total = l1 * a1 + a2
        inv = 1.0 / total
        out = acc_ref[cols(j), :] * (a1 * inv) + o_ret[cols(j), :].astype(F32) * (a2 * inv)
        low = out.astype(BF)
        att_ref[:, cols(j)] = jnp.transpose(low)
        grads = jnp.transpose(d_out[:, cols(j)]).astype(F32)
        st_ref[pl.ds(h, 1), :] = m + jnp.log2(total)
        st_ref[pl.ds(heads + h, 1), :] = jnp.sum(low.astype(F32) * grads, axis=0, keepdims=True)


def own_query_grads(
    sc, qn, do, st, knx, v, knp, vp, kne, ve, knf, vf, dq_ref, dk_ref, dv_ref
):
    step = pl.program_id(0)
    heads = pl.num_programs(0) * HB
    me, partner, near, far = around(sc)
    for j in range(HB):
        c = cols(j)
        p, ds = backward_unit(
            knx[:, c], v[:, c], qn[:, c], do[:, c],
            row(st, step * HB + j), row(st, heads + step * HB + j),
        )
        dq_ref[c, :] = dot(knx[:, c], ds, TN)
        dk_ref[:, c] = dot(ds, qn[:, c], NN)
        dv_ref[:, c] = dot(p.astype(BF), do[:, c], NN)
    for key_dev, kn, val in ((partner, knp, vp), (near, kne, ve), (far, knf, vf)):
        @pl.when(allowed(sc, me, key_dev))
        def _():
            for j in range(HB):
                c = cols(j)
                p, ds = backward_unit(
                    kn[:, c], val[:, c], qn[:, c], do[:, c],
                    row(st, step * HB + j), row(st, heads + step * HB + j),
                )
                dq_ref[c, :] += dot(kn[:, c], ds, TN)


def partner_query_grads(sc, qn, do, st, kne, ve, knf, vf, dq_ref, acc_ref):
    step = pl.program_id(0)
    heads = pl.num_programs(0) * HB
    me, partner, near, far = around(sc)
    acc_ref[...] = jnp.zeros_like(acc_ref)
    for key_dev, kn, val in ((near, kne, ve), (far, knf, vf)):
        @pl.when(allowed(sc, partner, key_dev))
        def _():
            for j in range(HB):
                c = cols(j)
                p, ds = backward_unit(
                    kn[:, c], val[:, c], qn[:, c], do[:, c],
                    row(st, step * HB + j), row(st, heads + step * HB + j),
                )
                acc_ref[c, :] += dot(kn[:, c], ds, TN)
    dq_ref[...] = acc_ref[...].astype(BF)


def key_units(sc, key_dev, kn, v, queries, dk_ref, dv_ref, step, heads):
    for query_dev, qn, do, st in queries:
        @pl.when(allowed(sc, query_dev, key_dev))
        def _():
            for j in range(HB):
                c = cols(j)
                p, ds = backward_unit(
                    kn[:, c], v[:, c], qn[:, c], do[:, c],
                    row(st, step * HB + j), row(st, heads + step * HB + j),
                )
                dk_ref[:, c] += dot(ds, qn[:, c], NN)
                dv_ref[:, c] += dot(p.astype(BF), do[:, c], NN)


def partner_key_grads(
    sc, g, knp, vp, qe, doe, ste, qf, dof, stf, dk_ref, dv_ref, qne, qnf, dka, dva
):
    step = pl.program_id(0)
    heads = pl.num_programs(0) * HB
    me, partner, near, far = around(sc)
    for j in range(HB):
        qne[:, cols(j)] = normed(qe[:, cols(j)], g[0:1, :])
        qnf[:, cols(j)] = normed(qf[:, cols(j)], g[0:1, :])
    dka[...] = jnp.zeros_like(dka)
    dva[...] = jnp.zeros_like(dva)
    key_units(
        sc, partner, knp, vp, ((near, qne, doe, ste), (far, qnf, dof, stf)), dka, dva, step, heads
    )
    dk_ref[...] = dka[...].astype(BF)
    dv_ref[...] = dva[...].astype(BF)


def own_key_grads(
    sc, knx, v, qnp, dop, stp, qne, doe, ste, qnf, dof, stf, dk0, dv0, dk_ref, dv_ref
):
    step = pl.program_id(0)
    heads = pl.num_programs(0) * HB
    me, partner, near, far = around(sc)
    dk_ref[...] = dk0[...]
    dv_ref[...] = dv0[...]
    key_units(
        sc, me, knx, v,
        ((partner, qnp, dop, stp), (near, qne, doe, ste), (far, qnf, dof, stf)),
        dk_ref, dv_ref, step, heads,
    )


def finish(g, dqt, dqr, dk, dkr, dv, dvr, q, k, dq_out, dk_out, dv_out):
    scale = 1.0 / math.sqrt(HD)
    for j in range(HB):
        c = cols(j)
        dq = jnp.transpose(dqt[c, :] + dqr[c, :].astype(F32)) * scale
        dq_out[:, c] = denormed(q[:, c], g[0:1, :], dq)
        dk_out[:, c] = denormed(k[:, c], g[1:2, :], (dk[:, c] + dkr[:, c].astype(F32)) * scale)
        dv_out[:, c] = (dv[:, c] + dvr[:, c].astype(F32)).astype(BF)


WIDE = "wide"
TALL = "tall"
FULL = "full"


def spec(kind, arr):
    if kind == WIDE:
        return pl.BlockSpec((ROWS, HB * HD), lambda i, *_: (0, i))
    if kind == TALL:
        return pl.BlockSpec((HB * HD, ROWS), lambda i, *_: (i, 0))
    return pl.BlockSpec(arr.shape, lambda i, *_: (0,) * len(arr.shape))


def run(name, body, scalars, ins, outs, scratch=(), units=1):
    features = next(a.shape[1] for kind, a in ins if kind == WIDE)
    shapes = [jax.ShapeDtypeStruct(s, d) for _, s, d in outs]
    grid_spec = pltpu.PrefetchScalarGridSpec(
        num_scalar_prefetch=len(scalars),
        grid=(features // (HB * HD),),
        in_specs=[spec(kind, a) for kind, a in ins],
        out_specs=[spec(o[0], s) for o, s in zip(outs, shapes)],
        scratch_shapes=list(scratch),
    )
    heads = features // HD
    flops = units * heads * 6 * 2 * ROWS * ROWS * HD
    return pl.pallas_call(
        body,
        name=name,
        grid_spec=grid_spec,
        out_shape=shapes,
        cost_estimate=pl.CostEstimate(
            flops=flops, transcendentals=units * heads * ROWS * ROWS, bytes_accessed=4 << 20
        ),
        compiler_params=pltpu.CompilerParams(
            dimension_semantics=("arbitrary",), vmem_limit_bytes=24 << 20
        ),
    )(*scalars, *[a for _, a in ins])


def after(values, *others):
    out = lax.optimization_barrier(tuple(values) + tuple(others))
    return out[: len(values)]


def local(q_raw, k_raw, values_in, d_out, gains, tile_device, neighbours):
    count = lax.axis_size("ctx")
    inner = [(d, d ^ 1) for d in range(count)]
    outer = []
    for d in range(1, count - 1, 2):
        outer += [(d, d + 1), (d + 1, d)]
    q, k, v, do = q_raw[0], k_raw[0], values_in[0], d_out[0]
    features = q.shape[1]
    heads = features // HD

    def across(value):
        return lax.ppermute(value, "ctx", inner)

    def beyond(value):
        return lax.ppermute(value, "ctx", outer)

    kp, vp, ke, ve = across(k), across(v), beyond(k), beyond(v)
    g = lax.all_gather(gains, "fsdp", axis=1, tiled=True)
    scalars = jnp.concatenate(
        [
            jnp.stack([lax.axis_index("ctx"), jnp.int32(count)]).astype(jnp.int32),
            tile_device,
            neighbours.reshape(-1),
        ]
    )
    q1, do1 = after((q, do), kp, vp)
    qp, dop = across(q1), across(do1)
    kf, vf = beyond(kp), beyond(vp)
    q2, do2 = after((q, do), kf, vf)
    qe, doe = beyond(q2), beyond(do2)
    qp3, dop3 = after((qp, dop), qe, doe)
    qf, dof = beyond(qp3), beyond(dop3)

    wide_bf = (WIDE, (ROWS, features), BF)
    wide_f = (WIDE, (ROWS, features), F32)
    tall_bf = (TALL, (features, ROWS), BF)
    tall_f = (TALL, (features, ROWS), F32)
    stats = (FULL, (2 * heads, ROWS), F32)
    rows_scratch = pltpu.VMEM((HB, 1, ROWS), F32)
    acc_t = pltpu.VMEM((HB * HD, ROWS), F32)
    acc_w = pltpu.VMEM((ROWS, HB * HD), F32)

    def wide(*arrays):
        return [(WIDE, a) for a in arrays]

    op, mlp, kne, knf, qnp = run(
        "partner_forward", partner_forward, (scalars,),
        [(FULL, g)] + wide(qp, ke, ve, kf, vf),
        [tall_bf, stats, wide_bf, wide_bf, wide_bf],
        (rows_scratch, rows_scratch, acc_t), 1,
    )
    o_ret, ml_ret = across(op), across(mlp)
    acc, ml, qnx, knx, knp = run(
        "own_forward", own_forward, (scalars,),
        [(FULL, g)] + wide(q, k, v, kp, vp, kne, ve, knf, vf),
        [tall_f, stats, wide_bf, wide_bf, wide_bf],
        (rows_scratch, rows_scratch), 2,
    )
    att, st = run(
        "merge", merge, (),
        [(TALL, acc), (FULL, ml), (TALL, o_ret), (FULL, ml_ret)] + wide(do),
        [wide_bf, stats],
    )
    stp, ste = across(st), beyond(st)
    stf = beyond(stp)
    dqt, dk0, dv0 = run(
        "own_query_grads", own_query_grads, (scalars,),
        wide(qnx, do) + [(FULL, st)] + wide(knx, v, knp, vp, kne, ve, knf, vf),
        [tall_f, wide_f, wide_f], (), 3,
    )
    (dqp,) = run(
        "partner_query_grads", partner_query_grads, (scalars,),
        wide(qnp, dop) + [(FULL, stp)] + wide(kne, ve, knf, vf),
        [tall_bf], (acc_t,), 1,
    )
    dqr = across(dqp)
    dkp, dvp, qne, qnf = run(
        "partner_key_grads", partner_key_grads, (scalars,),
        [(FULL, g)] + wide(knp, vp, qe, doe) + [(FULL, ste)] + wide(qf, dof) + [(FULL, stf)],
        [wide_bf, wide_bf, wide_bf, wide_bf], (acc_w, acc_w), 2,
    )
    dkr, dvr = across(dkp), across(dvp)
    dk1, dv1 = run(
        "own_key_grads", own_key_grads, (scalars,),
        wide(knx, v, qnp, dop) + [(FULL, stp)] + wide(qne, doe) + [(FULL, ste)]
        + wide(qnf, dof) + [(FULL, stf)] + wide(dk0, dv0),
        [wide_f, wide_f], (), 3,
    )
    dq_out, dk_out, dv_out = run(
        "finish", finish, (),
        [(FULL, g), (TALL, dqt), (TALL, dqr)] + wide(dk1, dkr, dv1, dvr, q, k),
        [wide_bf, wide_bf, wide_bf],
    )
    return att[None], dq_out[None], dk_out[None], dv_out[None]


def solution(mesh):
    tokens = P("fsdp", "ctx", None)
    return jax.shard_map(
        local,
        mesh=mesh,
        in_specs=(tokens, tokens, tokens, tokens, P(None, "fsdp"), P(), P()),
        out_specs=(tokens, tokens, tokens, tokens),
        check_vma=False,
    )
```

```python
import math
from functools import partial

import jax
import jax.numpy as jnp
from jax import lax
from jax.experimental import pallas as pl
from jax.experimental.pallas import tpu as pltpu
from jax.sharding import PartitionSpec as P

EPSILON = 1e-06
ROWS = 256
HD = 128
HB = 4
DEPTH = 1
LOW = -1e30
COST = 20_000_000_000
SCALE = math.log2(math.e) / math.sqrt(128)
BF = jnp.bfloat16
F32 = jnp.float32

NT = (((1,), (1,)), ((), ()))
TN = (((0,), (0,)), ((), ()))
NN = (((1,), (0,)), ((), ()))


def dot(a, b, dims):
    return lax.dot_general(a, b, dims, preferred_element_type=F32)


def allowed(sc, query_dev, key_dev):
    count = sc[1]
    inside = jnp.logical_and(
        jnp.logical_and(query_dev >= 0, query_dev < count),
        jnp.logical_and(key_dev >= 0, key_dev < count),
    )

    def tile_at(dev):
        first = 2 * (jnp.clip(dev, 0, count - 1) // 2)
        return jnp.where(sc[2 + first] == dev, first, first + 1)

    query_tile, key_tile = tile_at(query_dev), tile_at(key_dev)
    base = 2 + count + query_tile * 6
    hit = sc[base] == key_tile
    for slot in range(1, 6):
        hit = jnp.logical_or(hit, sc[base + slot] == key_tile)
    return jnp.logical_and(inside, hit)


def around(sc):
    me = sc[0]
    odd = me % 2 == 1
    partner = jnp.where(odd, me - 1, me + 1)
    near = jnp.where(odd, me + 1, me - 1)
    far = jnp.where(odd, me + 2, me - 2)
    return me, partner, near, far


def normed(raw, gain_row):
    floats = raw.astype(F32)
    inverse = lax.rsqrt(jnp.mean(floats * floats, axis=1, keepdims=True) + EPSILON)
    return (floats * inverse * gain_row).astype(BF)


def denormed(raw, gain_row, upstream):
    floats = raw.astype(F32)
    inverse = lax.rsqrt(jnp.mean(floats * floats, axis=1, keepdims=True) + EPSILON)
    scaled = upstream * gain_row
    inner = jnp.mean(floats * scaled, axis=1, keepdims=True)
    return (inverse * scaled - floats * (inverse * inverse * inverse * inner)).astype(BF)


def cols(j):
    return slice(j * HD, (j + 1) * HD)


def emit(units):
    first, second = {}, {}
    for t in range(len(units) + DEPTH + 1):
        if t < len(units):
            first[t] = units[t][0]()
        u = t - DEPTH - 1
        if u >= 0:
            units[u][2](second.pop(u))
        u = t - DEPTH
        if 0 <= u < len(units):
            second[u] = units[u][1](first.pop(u))


def forward_units(permit, kn, v, qn, m_ref, l_ref, acc_ref):
    units = []
    for j in range(HB):
        def scores(c=cols(j)):
            return dot(kn[:, c], qn[:, c], NT)

        def weights(s, j=j):
            top = jnp.max(s, axis=0, keepdims=True) * SCALE
            if permit is not None:
                top = jnp.where(permit, top, LOW)
            new = jnp.maximum(m_ref[j], top)
            shrink = jnp.exp2(m_ref[j] - new)
            m_ref[j] = new
            if permit is not None:
                new = jnp.where(permit, new, -LOW)
            return shrink, jnp.exp2(s * SCALE - new).astype(BF)

        def mix(found, j=j, c=cols(j)):
            shrink, p = found
            both = jnp.concatenate([v[:, c], jnp.ones((ROWS, HD), BF)], axis=1)
            out = dot(both, p, TN)
            l_ref[j] = l_ref[j] * shrink + out[HD : HD + 1]
            acc_ref[c, :] = acc_ref[c, :] * shrink + out[:HD]

        units.append((scores, weights, mix))
    return units


def backward_units(permit, kn, v, qn, do, st, use, first=None, heads=None, base=0):
    if heads is None:
        heads = pl.num_programs(0) * HB
    if first is None:
        first = pl.program_id(0) * HB
    units = []
    for j in range(HB):
        def scores(c=cols(j)):
            return dot(kn[:, c], qn[:, c], NT), dot(v[:, c], do[:, c], NT)

        def weights(found, h=base + first + j):
            s, dp = found
            lse = st[pl.ds(h, 1), :]
            if permit is not None:
                lse = jnp.where(permit, lse, -LOW)
            p = jnp.exp2(s * SCALE - lse)
            return p.astype(BF), (p * (dp - st[pl.ds(heads + h, 1), :])).astype(BF)

        units.append((scores, weights, partial(use, cols(j))))
    return units


def query_use(kn, dq_ref, c, found):
    dq_ref[c, :] += dot(kn[:, c], found[1], TN)


def key_use(qn, do, dk_ref, dv_ref, c, found):
    dk_ref[:, c] += dot(found[1], qn[:, c], NN)
    dv_ref[:, c] += dot(found[0], do[:, c], NN)


def clear(*refs):
    for ref in refs:
        ref[...] = jnp.zeros_like(ref)


def put_rows(ref, half, rows_ref):
    step = pl.program_id(0)
    heads = pl.num_programs(0) * HB
    for j in range(HB):
        ref[pl.ds(half * heads + step * HB + j, 1), :] = rows_ref[j]


def get_rows(ref, half, rows_ref):
    step = pl.program_id(0)
    heads = pl.num_programs(0) * HB
    for j in range(HB):
        rows_ref[j] = ref[pl.ds(half * heads + step * HB + j, 1), :]


def prepare(g, q, k, do, qn, kn, do_out):
    for j in range(HB):
        c = cols(j)
        qn[:, c] = normed(q[:, c], g[0:1, :])
        kn[:, c] = normed(k[:, c], g[1:2, :])
    do_out[...] = do[...]


def own_forward(
    sc, g, qn, knx, v, kp, vp, ke, ve, do, acc_ref, ml_ref, knp, kne, qn_out, do_out,
    m_ref, l_ref,
):
    me, partner, near, far = around(sc)
    qn_out[...] = qn[...]
    do_out[...] = do[...]
    for j in range(HB):
        c = cols(j)
        knp[:, c] = normed(kp[:, c], g[1:2, :])
        kne[:, c] = normed(ke[:, c], g[1:2, :])
    m_ref[...] = jnp.full_like(m_ref, LOW)
    clear(l_ref, acc_ref)
    emit(
        forward_units(None, knx, v, qn, m_ref, l_ref, acc_ref)
        + forward_units(allowed(sc, me, partner), knp, vp, qn, m_ref, l_ref, acc_ref)
        + forward_units(allowed(sc, me, near), kne, ve, qn, m_ref, l_ref, acc_ref)
    )
    put_rows(ml_ref, 0, m_ref)
    put_rows(ml_ref, 1, l_ref)


def partner_forward(sc, g, qn, kne, ve, kf, vf, o_ref, ml_ref, knf, m_ref, l_ref, acc_ref):
    me, partner, near, far = around(sc)
    for j in range(HB):
        knf[:, cols(j)] = normed(kf[:, cols(j)], g[1:2, :])
    m_ref[...] = jnp.full_like(m_ref, LOW)
    clear(l_ref, acc_ref)
    emit(
        forward_units(allowed(sc, partner, near), kne, ve, qn, m_ref, l_ref, acc_ref)
        + forward_units(allowed(sc, partner, far), knf, vf, qn, m_ref, l_ref, acc_ref)
    )
    put_rows(ml_ref, 0, m_ref)
    put_rows(ml_ref, 1, l_ref)
    for j in range(HB):
        total = l_ref[j]
        share = jnp.where(total > 0.0, 1.0 / jnp.where(total > 0.0, total, 1.0), 0.0)
        o_ref[cols(j), :] = (acc_ref[cols(j), :] * share).astype(BF)


def own_forward_far(sc, qn, knf, vf, acc0, ml0, acc_ref, ml_ref, m_ref, l_ref):
    me, partner, near, far = around(sc)
    get_rows(ml0, 0, m_ref)
    get_rows(ml0, 1, l_ref)
    acc_ref[...] = acc0[...]
    emit(forward_units(allowed(sc, me, far), knf, vf, qn, m_ref, l_ref, acc_ref))
    put_rows(ml_ref, 0, m_ref)
    put_rows(ml_ref, 1, l_ref)


def merge(acc_ref, ml_ref, o_ret, ml_ret, d_out, att_ref, st_ref):
    step = pl.program_id(0)
    heads = pl.num_programs(0) * HB
    for j in range(HB):
        h = step * HB + j
        m1, l1 = ml_ref[pl.ds(h, 1), :], ml_ref[pl.ds(heads + h, 1), :]
        m2, l2 = ml_ret[pl.ds(h, 1), :], ml_ret[pl.ds(heads + h, 1), :]
        m = jnp.maximum(m1, m2)
        a1 = jnp.exp2(m1 - m)
        a2 = jnp.exp2(m2 - m) * l2
        total = l1 * a1 + a2
        inv = 1.0 / total
        out = acc_ref[cols(j), :] * (a1 * inv) + o_ret[cols(j), :].astype(F32) * (a2 * inv)
        low = out.astype(BF)
        att_ref[:, cols(j)] = jnp.transpose(low)
        grads = jnp.transpose(d_out[:, cols(j)]).astype(F32)
        st_ref[pl.ds(h, 1), :] = m + jnp.log2(total)
        st_ref[pl.ds(heads + h, 1), :] = jnp.sum(low.astype(F32) * grads, axis=0, keepdims=True)


def own_query_grads(
    sc, qn, do, st, knx, v, knp, vp, kne, ve, knf, vf, dq_ref, dk_ref, dv_ref
):
    me, partner, near, far = around(sc)
    clear(dq_ref, dk_ref, dv_ref)

    def both(c, found):
        query_use(knx, dq_ref, c, found)
        key_use(qn, do, dk_ref, dv_ref, c, found)

    units = backward_units(None, knx, v, qn, do, st, both)
    for dev, kn, val in ((partner, knp, vp), (near, kne, ve), (far, knf, vf)):
        use = partial(query_use, kn, dq_ref)
        units += backward_units(allowed(sc, me, dev), kn, val, qn, do, st, use)
    emit(units)


def partner_query_grads(sc, qn, do, st, kne, ve, knf, vf, _, dq_ref, *rest):
    acc_ref = rest[-1]
    me, partner, near, far = around(sc)
    for chunk, both in enumerate(rest[:-1]):
        @pl.when(pl.program_id(0) == chunk)
        def _(both=both):
            both[:ROWS] = qn[...]
            both[ROWS:] = do[...]

    clear(acc_ref)
    units = []
    for dev, kn, val in ((near, kne, ve), (far, knf, vf)):
        use = partial(query_use, kn, acc_ref)
        units += backward_units(allowed(sc, partner, dev), kn, val, qn, do, st, use)
    emit(units)
    dq_ref[...] = acc_ref[...].astype(BF)


def near_key_grads(
    sc, knx, v, qnp, dop, stp, knp, vp, qne, doe, ste, dk0, dv0, _,
    dkx, dvx, dkp, dvp,
):
    me, partner, near, far = around(sc)
    dkx[...] = dk0[...]
    dvx[...] = dv0[...]
    clear(dkp, dvp)
    emit(
        backward_units(
            allowed(sc, partner, me), knx, v, qnp, dop, stp, partial(key_use, qnp, dop, dkx, dvx)
        )
        + backward_units(
            allowed(sc, near, me), knx, v, qne, doe, ste, partial(key_use, qne, doe, dkx, dvx)
        )
        + backward_units(
            allowed(sc, near, partner), knp, vp, qne, doe, ste,
            partial(key_use, qne, doe, dkp, dvp),
        )
    )


def partner_far_grads(chunk, heads, sc, knp, vp, both, st, dk0, dv0, _, out, dk, dv):
    me, partner, near, far = around(sc)
    dk[...] = dk0[...]
    dv[...] = dv0[...]
    qn, do = both.at[pl.ds(0, ROWS)], both.at[pl.ds(ROWS, ROWS)]
    emit(
        backward_units(
            allowed(sc, far, partner), knp, vp, qn, do, st, partial(key_use, qn, do, dk, dv),
            chunk * HB, heads, 2 * heads,
        )
    )
    out[:ROWS] = dk[...].astype(BF)
    out[ROWS:] = dv[...].astype(BF)


def own_far_grads(chunk, heads, sc, knx, v, both, st, dk0, dv0, _, dk, dv):
    me, partner, near, far = around(sc)
    dk[...] = dk0[...]
    dv[...] = dv0[...]
    qn, do = both.at[pl.ds(0, ROWS)], both.at[pl.ds(ROWS, ROWS)]
    emit(
        backward_units(
            allowed(sc, far, me), knx, v, qn, do, st, partial(key_use, qn, do, dk, dv),
            chunk * HB, heads, 2 * heads,
        )
    )


def finish_queries(g, dqt, dqr, q, _, dq_out):
    scale = 1.0 / math.sqrt(HD)
    for j in range(HB):
        c = cols(j)
        dq = jnp.transpose(dqt[c, :] + dqr[c, :].astype(F32)) * scale
        dq_out[:, c] = denormed(q[:, c], g[0:1, :], dq)


def finish_keys(g, k, *refs):
    dk_out, dv_out = refs[-2:]
    scale = 1.0 / math.sqrt(HD)
    for chunk in range((len(refs) - 2) // 3):
        dk, dv, back = refs[3 * chunk : 3 * chunk + 3]

        @pl.when(pl.program_id(0) == chunk)
        def _(dk=dk, dv=dv, back=back):
            for j in range(HB):
                c = cols(j)
                total = (dk[:, c] + back[:ROWS, c].astype(F32)) * scale
                dk_out[:, c] = denormed(k[:, c], g[1:2, :], total)
            dv_out[...] = (dv[...] + back[ROWS:].astype(F32)).astype(BF)


WIDE = "wide"
TALL = "tall"
FULL = "full"
ORDER = "order"


def spec(kind, arr):
    if kind == WIDE:
        return pl.BlockSpec((ROWS, HB * HD), lambda i, *_: (0, i))
    if kind == TALL:
        return pl.BlockSpec((HB * HD, ROWS), lambda i, *_: (i, 0))
    if isinstance(kind, int):
        return pl.BlockSpec((ROWS, HB * HD), lambda i, *_: (0, kind))
    if kind == ORDER:
        return pl.BlockSpec(memory_space=pl.ANY)
    return pl.BlockSpec(arr.shape, lambda i, *_: (0,) * len(arr.shape))


def run(body, scalars, ins, outs, scratch=(), steps=None, name=None):
    if steps is None:
        steps = next(a.shape[1] for kind, a in ins if kind == WIDE) // (HB * HD)
    shapes = [jax.ShapeDtypeStruct(s, d) for _, s, d in outs]
    grid_spec = pltpu.PrefetchScalarGridSpec(
        num_scalar_prefetch=len(scalars),
        grid=(steps,),
        in_specs=[spec(kind, a) for kind, a in ins],
        out_specs=[spec(o[0], s) for o, s in zip(outs, shapes)],
        scratch_shapes=list(scratch),
    )
    return pl.pallas_call(
        body,
        name=name or body.__name__,
        grid_spec=grid_spec,
        out_shape=shapes,
        cost_estimate=pl.CostEstimate(flops=COST, transcendentals=0, bytes_accessed=COST),
        compiler_params=pltpu.CompilerParams(
            dimension_semantics=("arbitrary",), vmem_limit_bytes=32 << 20
        ),
    )(*scalars, *[a for _, a in ins])


def local(q_raw, k_raw, values_in, d_out, gains, tile_device, neighbours):
    count = lax.axis_size("ctx")
    inner = [(d, d ^ 1) for d in range(count)]
    outer = []
    for d in range(1, count - 1, 2):
        outer += [(d, d + 1), (d + 1, d)]
    q, k, v, do = q_raw[0], k_raw[0], values_in[0], d_out[0]
    features = q.shape[1]
    heads = features // HD

    def across(*values):
        return [lax.ppermute(value, "ctx", inner) for value in values]

    def beyond(*values):
        return [lax.ppermute(value, "ctx", outer) for value in values]

    wide_bf = (WIDE, (ROWS, features), BF)
    wide_f = (WIDE, (ROWS, features), F32)
    tall_bf = (TALL, (features, ROWS), BF)
    tall_f = (TALL, (features, ROWS), F32)
    stats = (FULL, (2 * heads, ROWS), F32)
    row_s = pltpu.VMEM((HB, 1, ROWS), F32)
    acc_t = pltpu.VMEM((HB * HD, ROWS), F32)
    acc_w = pltpu.VMEM((ROWS, HB * HD), F32)

    def wide(*arrays):
        return [(WIDE, a) for a in arrays]

    kp, vp = across(k, v)
    ke, ve = beyond(k, v)
    g = lax.all_gather(gains, "fsdp", axis=1, tiled=True)
    place = jnp.stack([lax.axis_index("ctx"), jnp.int32(count)]).astype(jnp.int32)
    scalars = (jnp.concatenate([place, tile_device, neighbours.reshape(-1)]),)
    gain = [(FULL, g)]
    chunks = features // (HB * HD)
    pair = (FULL, (2 * ROWS, HB * HD), BF)
    part_f = (FULL, (ROWS, HB * HD), F32)

    qn, knx, do2 = run(prepare, (), gain + wide(q, k, do), [wide_bf] * 3)
    kf, vf = beyond(kp, vp)
    qnp, dop = across(qn, do2)

    acc, ml, knp, kne, qn3, do3 = run(
        own_forward, scalars, gain + wide(qn, knx, v, kp, vp, ke, ve, do),
        [tall_f, stats] + [wide_bf] * 4, (row_s, row_s),
    )
    qne, doe = beyond(qn3, do3)
    op, mlp, knf = run(
        partner_forward, scalars, gain + wide(qnp, kne, ve, kf, vf),
        [tall_bf, stats, wide_bf], (row_s, row_s, acc_t),
    )
    o_ret, ml_ret = across(op, mlp)
    acc, ml = run(
        own_forward_far, scalars,
        wide(qn, knf, vf) + [(TALL, acc), (FULL, ml)], [tall_f, stats], (row_s, row_s),
    )
    att, st = run(
        merge, (), [(TALL, acc), (FULL, ml), (TALL, o_ret), (FULL, ml_ret)] + wide(do),
        [wide_bf, stats],
    )
    (stp,) = across(st)
    (st2,) = beyond(jnp.concatenate([st, stp], axis=0))
    dqt, dk, dv = run(
        own_query_grads, scalars,
        wide(qn, do) + [(FULL, st)] + wide(knx, v, knp, vp, kne, ve, knf, vf),
        [tall_f, wide_f, wide_f],
    )
    dqp, *sent = run(
        partner_query_grads, scalars,
        wide(qnp, dop) + [(FULL, stp)] + wide(kne, ve, knf, vf) + [(ORDER, dqt)],
        [tall_bf] + [pair] * chunks, (acc_t,),
    )
    (dqr,) = across(dqp)
    far = beyond(*sent)
    dk, dv, dkp, dvp = run(
        near_key_grads, scalars,
        wide(knx, v, qnp, dop) + [(FULL, stp)] + wide(knp, vp, qne, doe) + [(FULL, st2)]
        + wide(dk, dv) + [(ORDER, dqp)],
        [wide_f] * 4,
    )
    last, back, own = dkp, [], []
    for i in range(chunks):
        out, _, _ = run(
            partial(partner_far_grads, i, heads), scalars,
            [(i, knp), (i, vp), (FULL, far[i]), (FULL, st2), (i, dkp), (i, dvp), (ORDER, last)],
            [pair, part_f, part_f], (), 1, "partner_far_grads",
        )
        back += across(out)
        dki, dvi = run(
            partial(own_far_grads, i, heads), scalars,
            [(i, knx), (i, v), (FULL, far[i]), (FULL, st2), (i, dk), (i, dv), (ORDER, out)],
            [part_f, part_f], (), 1, "own_far_grads",
        )
        own.append((dki, dvi))
        last = dki
    (dq_out,) = run(
        finish_queries, (), gain + [(TALL, dqt), (TALL, dqr)] + wide(q) + [(ORDER, last)],
        [wide_bf],
    )
    pieces = []
    for i in range(chunks):
        pieces += [(FULL, own[i][0]), (FULL, own[i][1]), (FULL, back[i])]
    dk_out, dv_out = run(finish_keys, (), gain + wide(k) + pieces, [wide_bf] * 2)
    return att[None], dq_out[None], dk_out[None], dv_out[None]


def solution(mesh):
    tokens = P("fsdp", "ctx", None)
    return jax.shard_map(
        local,
        mesh=mesh,
        in_specs=(tokens, tokens, tokens, tokens, P(None, "fsdp"), P(), P()),
        out_specs=(tokens, tokens, tokens, tokens),
        check_vma=False,
    )
```

```python
import math
from functools import partial

import jax
import jax.numpy as jnp
from jax import lax
from jax.experimental import pallas as pl
from jax.experimental.pallas import tpu as pltpu
from jax.sharding import PartitionSpec as P

EPSILON = 1e-06
ROWS = 256
HD = 128
HB = 4
DEPTH = 1
LOW = -1e30
COST = dict.fromkeys(
    (
        "partner_forward",
        "own_forward_far",
        "merge_stats",
        "partner_query_grads",
        "own_query_grads",
    ),
    0,
)
OTHER = 20_000_000_000
SCALE = math.log2(math.e) / math.sqrt(128)
BF = jnp.bfloat16
F32 = jnp.float32

NT = (((1,), (1,)), ((), ()))
TN = (((0,), (0,)), ((), ()))
NN = (((1,), (0,)), ((), ()))


def dot(a, b, dims):
    return lax.dot_general(a, b, dims, preferred_element_type=F32)


def allowed(sc, query_dev, key_dev):
    count = sc[1]
    inside = jnp.logical_and(
        jnp.logical_and(query_dev >= 0, query_dev < count),
        jnp.logical_and(key_dev >= 0, key_dev < count),
    )

    def tile_at(dev):
        first = 2 * (jnp.clip(dev, 0, count - 1) // 2)
        return jnp.where(sc[2 + first] == dev, first, first + 1)

    query_tile, key_tile = tile_at(query_dev), tile_at(key_dev)
    base = 2 + count + query_tile * 6
    hit = sc[base] == key_tile
    for slot in range(1, 6):
        hit = jnp.logical_or(hit, sc[base + slot] == key_tile)
    return jnp.logical_and(inside, hit)


def around(sc):
    me = sc[0]
    odd = me % 2 == 1
    partner = jnp.where(odd, me - 1, me + 1)
    near = jnp.where(odd, me + 1, me - 1)
    far = jnp.where(odd, me + 2, me - 2)
    return me, partner, near, far


def normed(raw, gain_row):
    floats = raw.astype(F32)
    inverse = lax.rsqrt(jnp.mean(floats * floats, axis=1, keepdims=True) + EPSILON)
    return (floats * inverse * gain_row).astype(BF)


def denormed(raw, gain_row, upstream):
    floats = raw.astype(F32)
    inverse = lax.rsqrt(jnp.mean(floats * floats, axis=1, keepdims=True) + EPSILON)
    scaled = upstream * gain_row
    inner = jnp.mean(floats * scaled, axis=1, keepdims=True)
    return (inverse * scaled - floats * (inverse * inverse * inverse * inner)).astype(BF)


def cols(j):
    return slice(j * HD, (j + 1) * HD)


def emit(units):
    first, second = {}, {}
    for t in range(len(units) + DEPTH + 1):
        if t < len(units):
            first[t] = units[t][0]()
        u = t - DEPTH - 1
        if u >= 0:
            units[u][2](second.pop(u))
        u = t - DEPTH
        if 0 <= u < len(units):
            second[u] = units[u][1](first.pop(u))


def forward_units(permit, kn, v, qn, m_ref, l_ref, acc_ref):
    units = []
    for j in range(HB):
        def scores(c=cols(j)):
            return dot(kn[:, c], qn[:, c], NT)

        def weights(s, j=j):
            top = jnp.max(s, axis=0, keepdims=True) * SCALE
            if permit is not None:
                top = jnp.where(permit, top, LOW)
            new = jnp.maximum(m_ref[j], top)
            shrink = jnp.exp2(m_ref[j] - new)
            m_ref[j] = new
            if permit is not None:
                new = jnp.where(permit, new, -LOW)
            return shrink, jnp.exp2(s * SCALE - new).astype(BF)

        def mix(found, j=j, c=cols(j)):
            shrink, p = found
            both = jnp.concatenate([v[:, c], jnp.ones((ROWS, HD), BF)], axis=1)
            out = dot(both, p, TN)
            l_ref[j] = l_ref[j] * shrink + out[HD : HD + 1]
            acc_ref[c, :] = acc_ref[c, :] * shrink + out[:HD]

        units.append((scores, weights, mix))
    return units


def backward_units(permit, kn, v, qn, do, st, use, half=0, first=None, heads=None):
    if heads is None:
        heads = pl.num_programs(0) * HB
    if first is None:
        first = pl.program_id(0) * HB
    base = 2 * half * heads
    units = []
    for j in range(HB):
        def scores(c=cols(j)):
            return dot(kn[:, c], qn[:, c], NT), dot(v[:, c], do[:, c], NT)

        def weights(found, h=base + first + j):
            s, dp = found
            lse = st[pl.ds(h, 1), :]
            if permit is not None:
                lse = jnp.where(permit, lse, -LOW)
            p = jnp.exp2(s * SCALE - lse)
            return p.astype(BF), (p * (dp - st[pl.ds(heads + h, 1), :])).astype(BF)

        units.append((scores, weights, partial(use, cols(j))))
    return units


def query_use(kn, dq_ref, c, found):
    dq_ref[c, :] += dot(kn[:, c], found[1], TN)


def key_use(qn, do, dk_ref, dv_ref, c, found):
    dk_ref[:, c] += dot(found[1], qn[:, c], NN)
    dv_ref[:, c] += dot(found[0], do[:, c], NN)


def clear(*refs):
    for ref in refs:
        ref[...] = jnp.zeros_like(ref)


def put_rows(ref, half, rows_ref):
    step = pl.program_id(0)
    heads = pl.num_programs(0) * HB
    for j in range(HB):
        ref[pl.ds(half * heads + step * HB + j, 1), :] = rows_ref[j]


def get_rows(ref, half, rows_ref):
    step = pl.program_id(0)
    heads = pl.num_programs(0) * HB
    for j in range(HB):
        rows_ref[j] = ref[pl.ds(half * heads + step * HB + j, 1), :]


def prepare(g, q, k, do, qn, kn, do_out):
    for j in range(HB):
        c = cols(j)
        qn[:, c] = normed(q[:, c], g[0:1, :])
        kn[:, c] = normed(k[:, c], g[1:2, :])
    do_out[...] = do[...]


def own_forward(
    sc, g, qn, knx, v, kp, vp, ke, ve, do, acc_ref, ml_ref, knp, kne, qn_out, do_out,
    m_ref, l_ref,
):
    me, partner, near, far = around(sc)
    qn_out[...] = qn[...]
    do_out[...] = do[...]
    for j in range(HB):
        c = cols(j)
        knp[:, c] = normed(kp[:, c], g[1:2, :])
        kne[:, c] = normed(ke[:, c], g[1:2, :])
    m_ref[...] = jnp.full_like(m_ref, LOW)
    clear(l_ref, acc_ref)
    emit(
        forward_units(None, knx, v, qn, m_ref, l_ref, acc_ref)
        + forward_units(allowed(sc, me, partner), knp, vp, qn, m_ref, l_ref, acc_ref)
        + forward_units(allowed(sc, me, near), kne, ve, qn, m_ref, l_ref, acc_ref)
    )
    put_rows(ml_ref, 0, m_ref)
    put_rows(ml_ref, 1, l_ref)


def delta_row(out, do):
    return jnp.sum(out * jnp.transpose(do).astype(F32), axis=0, keepdims=True)


def partner_forward(
    sc, g, qn, kne, ve, kf, vf, do, o_ref, ml_ref, knf, m_ref, l_ref, d_ref, acc_ref
):
    me, partner, near, far = around(sc)
    for j in range(HB):
        knf[:, cols(j)] = normed(kf[:, cols(j)], g[1:2, :])
    m_ref[...] = jnp.full_like(m_ref, LOW)
    clear(l_ref, acc_ref)
    emit(
        forward_units(allowed(sc, partner, near), kne, ve, qn, m_ref, l_ref, acc_ref)
        + forward_units(allowed(sc, partner, far), knf, vf, qn, m_ref, l_ref, acc_ref)
    )
    for j in range(HB):
        total = l_ref[j]
        share = jnp.where(total > 0.0, 1.0 / jnp.where(total > 0.0, total, 1.0), 0.0)
        out = acc_ref[cols(j), :] * share
        o_ref[cols(j), :] = out.astype(BF)
        d_ref[j] = delta_row(out, do[:, cols(j)])
    for index, rows in enumerate((m_ref, l_ref, d_ref)):
        put_rows(ml_ref, index, rows)


def own_forward_far(
    sc, qn, knf, vf, do, acc0, ml0, mlp, acc_ref, st_ref, m_ref, l_ref, d_ref
):
    me, partner, near, far = around(sc)

    @pl.when(pl.program_id(0) == 0)
    def _():
        st_ref[mlp.shape[0] :, :] = mlp[...]

    get_rows(ml0, 0, m_ref)
    get_rows(ml0, 1, l_ref)
    acc_ref[...] = acc0[...]
    emit(forward_units(allowed(sc, me, far), knf, vf, qn, m_ref, l_ref, acc_ref))
    for j in range(HB):
        d_ref[j] = delta_row(acc_ref[cols(j), :] * (1.0 / l_ref[j]), do[:, cols(j)])
    for index, rows in enumerate((m_ref, l_ref, d_ref)):
        put_rows(st_ref, index, rows)


def weights_of(first, second, heads):
    m1, l1 = first[:heads], first[heads : 2 * heads]
    m2, l2 = second[:heads], second[heads : 2 * heads]
    m = jnp.maximum(m1, m2)
    w1, w2 = l1 * jnp.exp2(m1 - m), l2 * jnp.exp2(m2 - m)
    total = w1 + w2
    return w1 / total, w2 / total, m + jnp.log2(total)


def merge_stats(mine, got, o_ref, st_ref, sh_ref, o_out):
    o_out[...] = o_ref[...]

    @pl.when(pl.program_id(0) == 0)
    def _():
        size = mine.shape[0] // 2
        heads = size // 3
        both = ((mine[:size], got[size:]), (got[:size], mine[size:]))
        for half, (first, second) in enumerate(both):
            w1, w2, lse = weights_of(first, second, heads)
            base = 2 * half * heads
            st_ref[base : base + heads] = lse
            st_ref[base + heads : base + 2 * heads] = (
                w1 * first[2 * heads :] + w2 * second[2 * heads :]
            )
            if half == 0:
                total = first[heads : 2 * heads]
                sh_ref[:heads] = w1 / total
                sh_ref[heads:] = w2


def merge(acc_ref, sh, o_ret, _, att_ref):
    step = pl.program_id(0)
    heads = pl.num_programs(0) * HB
    for j in range(HB):
        c, h = cols(j), step * HB + j
        w1, w2 = sh[pl.ds(h, 1), :], sh[pl.ds(heads + h, 1), :]
        out = acc_ref[c, :] * w1 + o_ret[c, :].astype(F32) * w2
        att_ref[:, c] = jnp.transpose(out.astype(BF))


def stack(both, qn, do):
    @pl.when(pl.program_id(0) == 0)
    def _():
        both[:ROWS] = qn[...]
        both[ROWS:] = do[...]


def own_query_grads(
    sc, qn, do, st, knx, v, knp, vp, kne, ve, knf, vf, qs, ds, _, dq_ref, dk_ref, dv_ref, both_out
):
    me, partner, near, far = around(sc)
    stack(both_out, qs, ds)
    clear(dq_ref, dk_ref, dv_ref)

    def both(c, found):
        query_use(knx, dq_ref, c, found)
        key_use(qn, do, dk_ref, dv_ref, c, found)

    units = backward_units(None, knx, v, qn, do, st, both)
    for dev, kn, val in ((partner, knp, vp), (near, kne, ve), (far, knf, vf)):
        use = partial(query_use, kn, dq_ref)
        units += backward_units(allowed(sc, me, dev), kn, val, qn, do, st, use)
    emit(units)


def partner_query_grads(
    sc, qn, do, st, kne, ve, knf, vf, qs, ds, dq_ref, both_out, acc_ref
):
    me, partner, near, far = around(sc)
    stack(both_out, qs, ds)
    clear(acc_ref)
    units = []
    for dev, kn, val in ((near, kne, ve), (far, knf, vf)):
        use = partial(query_use, kn, acc_ref)
        units += backward_units(allowed(sc, partner, dev), kn, val, qn, do, st, use, 1)
    emit(units)
    dq_ref[...] = acc_ref[...].astype(BF)


def near_key_grads(
    sc, knx, v, qnp, dop, st, knp, vp, qne, doe, ste, dk0, dv0, qs, ds, _,
    dkx, dvx, dkp, dvp, both_out,
):
    me, partner, near, far = around(sc)
    stack(both_out, qs, ds)
    dkx[...] = dk0[...]
    dvx[...] = dv0[...]
    clear(dkp, dvp)
    own = partial(key_use, qnp, dop, dkx, dvx)
    use = partial(key_use, qne, doe, dkx, dvx)
    back = partial(key_use, qne, doe, dkp, dvp)
    emit(
        backward_units(allowed(sc, partner, me), knx, v, qnp, dop, st, own, 1)
        + backward_units(allowed(sc, near, me), knx, v, qne, doe, ste, use)
        + backward_units(allowed(sc, near, partner), knp, vp, qne, doe, ste, back)
    )


def partner_far_grads(chunk, heads, sc, knp, vp, both, st, dk0, dv0, _, out, dk, dv):
    me, partner, near, far = around(sc)
    dk[...] = dk0[...]
    dv[...] = dv0[...]
    qn, do = both.at[pl.ds(0, ROWS)], both.at[pl.ds(ROWS, ROWS)]
    emit(
        backward_units(
            allowed(sc, far, partner), knp, vp, qn, do, st, partial(key_use, qn, do, dk, dv),
            1, chunk * HB, heads,
        )
    )
    out[:ROWS] = dk[...].astype(BF)
    out[ROWS:] = dv[...].astype(BF)


def own_far_grads(chunk, heads, sc, knx, v, both, st, dk0, dv0, _, dk, dv):
    me, partner, near, far = around(sc)
    dk[...] = dk0[...]
    dv[...] = dv0[...]
    qn, do = both.at[pl.ds(0, ROWS)], both.at[pl.ds(ROWS, ROWS)]
    emit(
        backward_units(
            allowed(sc, far, me), knx, v, qn, do, st, partial(key_use, qn, do, dk, dv),
            1, chunk * HB, heads,
        )
    )


def finish_queries(g, dqt, dqr, q, _, dq_out):
    scale = 1.0 / math.sqrt(HD)
    for j in range(HB):
        c = cols(j)
        dq = jnp.transpose(dqt[c, :] + dqr[c, :].astype(F32)) * scale
        dq_out[:, c] = denormed(q[:, c], g[0:1, :], dq)


def finish_keys(g, k, *refs):
    dk_out, dv_out = refs[-2:]
    scale = 1.0 / math.sqrt(HD)
    for chunk in range((len(refs) - 2) // 3):
        dk, dv, back = refs[3 * chunk : 3 * chunk + 3]

        @pl.when(pl.program_id(0) == chunk)
        def _(dk=dk, dv=dv, back=back):
            for j in range(HB):
                c = cols(j)
                total = (dk[:, c] + back[:ROWS, c].astype(F32)) * scale
                dk_out[:, c] = denormed(k[:, c], g[1:2, :], total)
            dv_out[...] = (dv[...] + back[ROWS:].astype(F32)).astype(BF)


WIDE = "wide"
TALL = "tall"
FULL = "full"
ORDER = "order"


def spec(kind, arr):
    if kind == WIDE:
        return pl.BlockSpec((ROWS, HB * HD), lambda i, *_: (0, i))
    if kind == TALL:
        return pl.BlockSpec((HB * HD, ROWS), lambda i, *_: (i, 0))
    if isinstance(kind, int):
        return pl.BlockSpec((ROWS, HB * HD), lambda i, *_: (0, kind))
    if kind == ORDER:
        return pl.BlockSpec(memory_space=pl.ANY)
    return pl.BlockSpec(arr.shape, lambda i, *_: (0,) * len(arr.shape))


def run(body, scalars, ins, outs, scratch=(), steps=None, name=None):
    if steps is None:
        steps = next(a.shape[1] for kind, a in ins if kind == WIDE) // (HB * HD)
    shapes = [jax.ShapeDtypeStruct(s, d) for _, s, d in outs]
    grid_spec = pltpu.PrefetchScalarGridSpec(
        num_scalar_prefetch=len(scalars),
        grid=(steps,),
        in_specs=[spec(kind, a) for kind, a in ins],
        out_specs=[spec(o[0], s) for o, s in zip(outs, shapes)],
        scratch_shapes=list(scratch),
    )
    return pl.pallas_call(
        body,
        name=name or body.__name__,
        grid_spec=grid_spec,
        out_shape=shapes,
        cost_estimate=pl.CostEstimate(
            flops=COST.get(name or body.__name__, OTHER),
            transcendentals=0,
            bytes_accessed=COST.get(name or body.__name__, OTHER),
        ),
        compiler_params=pltpu.CompilerParams(
            dimension_semantics=("arbitrary",), vmem_limit_bytes=32 << 20
        ),
    )(*scalars, *[a for _, a in ins])


def local(q_raw, k_raw, values_in, d_out, gains, tile_device, neighbours):
    count = lax.axis_size("ctx")
    inner = [(d, d ^ 1) for d in range(count)]
    outer = []
    for d in range(1, count - 1, 2):
        outer += [(d, d + 1), (d + 1, d)]
    q, k, v, do = q_raw[0], k_raw[0], values_in[0], d_out[0]
    features = q.shape[1]
    heads = features // HD

    def across(*values):
        return [lax.ppermute(value, "ctx", inner) for value in values]

    def beyond(*values):
        return [lax.ppermute(value, "ctx", outer) for value in values]

    wide_bf = (WIDE, (ROWS, features), BF)
    wide_f = (WIDE, (ROWS, features), F32)
    tall_bf = (TALL, (features, ROWS), BF)
    tall_f = (TALL, (features, ROWS), F32)
    stats = (FULL, (2 * heads, ROWS), F32)
    row_s = pltpu.VMEM((HB, 1, ROWS), F32)
    acc_t = pltpu.VMEM((HB * HD, ROWS), F32)
    acc_w = pltpu.VMEM((ROWS, HB * HD), F32)

    def wide(*arrays):
        return [(WIDE, a) for a in arrays]

    kp, vp = across(k, v)
    ke, ve = beyond(k, v)
    g = lax.all_gather(gains, "fsdp", axis=1, tiled=True)
    place = jnp.stack([lax.axis_index("ctx"), jnp.int32(count)]).astype(jnp.int32)
    scalars = (jnp.concatenate([place, tile_device, neighbours.reshape(-1)]),)
    gain = [(FULL, g)]
    chunks = features // (HB * HD)
    pair = (FULL, (2 * ROWS, HB * HD), BF)
    part_f = (FULL, (ROWS, HB * HD), F32)

    qn, knx, do2 = run(prepare, (), gain + wide(q, k, do), [wide_bf] * 3)
    kf, vf = beyond(kp, vp)
    qnp, dop = across(qn, do2)

    acc, ml, knp, kne, qn3, do3 = run(
        own_forward, scalars, gain + wide(qn, knx, v, kp, vp, ke, ve, do),
        [tall_f, stats] + [wide_bf] * 4, (row_s, row_s),
    )
    qne, doe = beyond(qn3, do3)
    parts = (FULL, (3 * heads, ROWS), F32)
    op, mlp, knf = run(
        partner_forward, scalars, gain + wide(qnp, kne, ve, kf, vf, dop),
        [tall_bf, parts, wide_bf], (row_s, row_s, row_s, acc_t),
    )
    acc, mine = run(
        own_forward_far, scalars,
        wide(qn, knf, vf, do) + [(TALL, acc), (FULL, ml), (FULL, mlp)],
        [tall_f, (FULL, (6 * heads, ROWS), F32)], (row_s, row_s, row_s),
    )
    (got,) = across(mine)
    st, shares, op = run(
        merge_stats, (), [(FULL, mine), (FULL, got), (TALL, op)],
        [(FULL, (4 * heads, ROWS), F32), stats, tall_bf], (), chunks,
    )
    (ste,) = beyond(st)
    (o_ret,) = across(op)

    def send(i):
        return [(i, qnp), (i, dop)]

    dqp, sent0 = run(
        partner_query_grads, scalars,
        wide(qnp, dop) + [(FULL, st)] + wide(kne, ve, knf, vf) + send(0),
        [tall_bf, pair], (acc_t,),
    )
    (dqr,) = across(dqp)
    dqt, dk, dv, sent1 = run(
        own_query_grads, scalars,
        wide(qn, do) + [(FULL, st)] + wide(knx, v, knp, vp, kne, ve, knf, vf) + send(1)
        + [(ORDER, dqp)],
        [tall_f, wide_f, wide_f, pair],
    )
    dk, dv, dkp, dvp, sent2 = run(
        near_key_grads, scalars,
        wide(knx, v, qnp, dop) + [(FULL, st)] + wide(knp, vp, qne, doe) + [(FULL, ste)]
        + wide(dk, dv) + send(2) + [(ORDER, dqt)],
        [wide_f] * 4 + [pair],
    )
    far = beyond(sent0, sent1, sent2)
    (att,) = run(
        merge, (), [(TALL, acc), (FULL, shares), (TALL, o_ret), (ORDER, dkp)], [wide_bf], (), chunks,
    )
    last, back, own = att, [], []
    for i in range(chunks):
        out, _, _ = run(
            partial(partner_far_grads, i, heads), scalars,
            [(i, knp), (i, vp), (FULL, far[i]), (FULL, ste), (i, dkp), (i, dvp), (ORDER, last)],
            [pair, part_f, part_f], (), 1, "partner_far_grads",
        )
        back += across(out)
        dki, dvi = run(
            partial(own_far_grads, i, heads), scalars,
            [(i, knx), (i, v), (FULL, far[i]), (FULL, ste), (i, dk), (i, dv), (ORDER, out)],
            [part_f, part_f], (), 1, "own_far_grads",
        )
        own.append((dki, dvi))
        last = dki
        if i == 0:
            (dq_out,) = run(
                finish_queries, (),
                gain + [(TALL, dqt), (TALL, dqr)] + wide(q) + [(ORDER, last)], [wide_bf],
            )
            last = dq_out
    pieces = []
    for i in range(chunks):
        pieces += [(FULL, own[i][0]), (FULL, own[i][1]), (FULL, back[i])]
    dk_out, dv_out = run(finish_keys, (), gain + wide(k) + pieces, [wide_bf] * 2)
    return att[None], dq_out[None], dk_out[None], dv_out[None]


def solution(mesh):
    tokens = P("fsdp", "ctx", None)
    return jax.shard_map(
        local,
        mesh=mesh,
        in_specs=(tokens, tokens, tokens, tokens, P(None, "fsdp"), P(), P()),
        out_specs=(tokens, tokens, tokens, tokens),
        check_vma=False,
    )
```

```python
import math
from functools import partial

import jax
import jax.numpy as jnp
from jax import lax
from jax.experimental import pallas as pl
from jax.experimental.pallas import tpu as pltpu
from jax.sharding import PartitionSpec as P

EPSILON = 1e-06
ROWS = 256
HD = 128
HB = 4
DEPTH = 1
LOW = -1e30
COST = dict.fromkeys(
    (
        "partner_forward",
        "own_forward_far",
        "merge_stats",
        "partner_query_grads",
        "own_query_grads",
    ),
    0,
)
OTHER = 20_000_000_000
SCALE = math.log2(math.e) / math.sqrt(128)
BF = jnp.bfloat16
F32 = jnp.float32

NT = (((1,), (1,)), ((), ()))
TN = (((0,), (0,)), ((), ()))
NN = (((1,), (0,)), ((), ()))


def dot(a, b, dims):
    return lax.dot_general(a, b, dims, preferred_element_type=F32)


def allowed(sc, query_dev, key_dev):
    count = sc[1]
    inside = jnp.logical_and(
        jnp.logical_and(query_dev >= 0, query_dev < count),
        jnp.logical_and(key_dev >= 0, key_dev < count),
    )

    def tile_at(dev):
        first = 2 * (jnp.clip(dev, 0, count - 1) // 2)
        return jnp.where(sc[2 + first] == dev, first, first + 1)

    query_tile, key_tile = tile_at(query_dev), tile_at(key_dev)
    base = 2 + count + query_tile * 6
    hit = sc[base] == key_tile
    for slot in range(1, 6):
        hit = jnp.logical_or(hit, sc[base + slot] == key_tile)
    return jnp.logical_and(inside, hit)


def around(sc):
    me = sc[0]
    odd = me % 2 == 1
    partner = jnp.where(odd, me - 1, me + 1)
    near = jnp.where(odd, me + 1, me - 1)
    far = jnp.where(odd, me + 2, me - 2)
    return me, partner, near, far


def normed(raw, gain_row):
    floats = raw.astype(F32)
    inverse = lax.rsqrt(jnp.mean(floats * floats, axis=1, keepdims=True) + EPSILON)
    return (floats * inverse * gain_row).astype(BF)


def denormed(raw, gain_row, upstream):
    floats = raw.astype(F32)
    inverse = lax.rsqrt(jnp.mean(floats * floats, axis=1, keepdims=True) + EPSILON)
    scaled = upstream * gain_row
    inner = jnp.mean(floats * scaled, axis=1, keepdims=True)
    return (inverse * scaled - floats * (inverse * inverse * inverse * inner)).astype(BF)


def cols(j):
    return slice(j * HD, (j + 1) * HD)


def emit(units):
    first, second = {}, {}
    for t in range(len(units) + DEPTH + 1):
        if t < len(units):
            first[t] = units[t][0]()
        u = t - DEPTH - 1
        if u >= 0:
            units[u][2](second.pop(u))
        u = t - DEPTH
        if 0 <= u < len(units):
            second[u] = units[u][1](first.pop(u))


def forward_units(permit, kn, v, qn, m_ref, l_ref, acc_ref):
    units = []
    for j in range(HB):
        def scores(c=cols(j)):
            return dot(kn[:, c], qn[:, c], NT)

        def weights(s, j=j):
            top = jnp.max(s, axis=0, keepdims=True) * SCALE
            if permit is not None:
                top = jnp.where(permit, top, LOW)
            new = jnp.maximum(m_ref[j], top)
            shrink = jnp.exp2(m_ref[j] - new)
            m_ref[j] = new
            if permit is not None:
                new = jnp.where(permit, new, -LOW)
            return shrink, jnp.exp2(s * SCALE - new).astype(BF)

        def mix(found, j=j, c=cols(j)):
            shrink, p = found
            both = jnp.concatenate([v[:, c], jnp.ones((ROWS, HD), BF)], axis=1)
            out = dot(both, p, TN)
            l_ref[j] = l_ref[j] * shrink + out[HD : HD + 1]
            acc_ref[c, :] = acc_ref[c, :] * shrink + out[:HD]

        units.append((scores, weights, mix))
    return units


def backward_units(permit, kn, v, qn, do, st, use, half=0, first=None, heads=None):
    if heads is None:
        heads = pl.num_programs(0) * HB
    if first is None:
        first = pl.program_id(0) * HB
    base = 2 * half * heads
    units = []
    for j in range(HB):
        def scores(c=cols(j)):
            return dot(kn[:, c], qn[:, c], NT), dot(v[:, c], do[:, c], NT)

        def weights(found, h=base + first + j):
            s, dp = found
            lse = st[pl.ds(h, 1), :]
            if permit is not None:
                lse = jnp.where(permit, lse, -LOW)
            p = jnp.exp2(s * SCALE - lse)
            return p.astype(BF), (p * (dp - st[pl.ds(heads + h, 1), :])).astype(BF)

        units.append((scores, weights, partial(use, cols(j))))
    return units


def query_use(kn, dq_ref, c, found):
    dq_ref[c, :] += dot(kn[:, c], found[1], TN)


def key_use(qn, do, dk_ref, dv_ref, c, found):
    dk_ref[:, c] += dot(found[1], qn[:, c], NN)
    dv_ref[:, c] += dot(found[0], do[:, c], NN)


def clear(*refs):
    for ref in refs:
        ref[...] = jnp.zeros_like(ref)


def put_rows(ref, half, rows_ref):
    step = pl.program_id(0)
    heads = pl.num_programs(0) * HB
    for j in range(HB):
        ref[pl.ds(half * heads + step * HB + j, 1), :] = rows_ref[j]


def get_rows(ref, half, rows_ref):
    step = pl.program_id(0)
    heads = pl.num_programs(0) * HB
    for j in range(HB):
        rows_ref[j] = ref[pl.ds(half * heads + step * HB + j, 1), :]


def prepare(g, q, k, do, qn, kn, do_out):
    for j in range(HB):
        c = cols(j)
        qn[:, c] = normed(q[:, c], g[0:1, :])
        kn[:, c] = normed(k[:, c], g[1:2, :])
    do_out[...] = do[...]


def own_forward(
    sc, g, qn, knx, v, kp, vp, ke, ve, do, acc_ref, ml_ref, knp, kne, qn_out, do_out,
    m_ref, l_ref,
):
    me, partner, near, far = around(sc)
    qn_out[...] = qn[...]
    do_out[...] = do[...]
    for j in range(HB):
        c = cols(j)
        knp[:, c] = normed(kp[:, c], g[1:2, :])
        kne[:, c] = normed(ke[:, c], g[1:2, :])
    m_ref[...] = jnp.full_like(m_ref, LOW)
    clear(l_ref, acc_ref)
    emit(
        forward_units(None, knx, v, qn, m_ref, l_ref, acc_ref)
        + forward_units(allowed(sc, me, partner), knp, vp, qn, m_ref, l_ref, acc_ref)
        + forward_units(allowed(sc, me, near), kne, ve, qn, m_ref, l_ref, acc_ref)
    )
    put_rows(ml_ref, 0, m_ref)
    put_rows(ml_ref, 1, l_ref)


def delta_row(out, do):
    return jnp.sum(out * jnp.transpose(do).astype(F32), axis=0, keepdims=True)


def partner_forward(
    sc, g, qn, kne, ve, kf, vf, do, o_ref, ml_ref, knf, m_ref, l_ref, d_ref, acc_ref
):
    me, partner, near, far = around(sc)
    for j in range(HB):
        knf[:, cols(j)] = normed(kf[:, cols(j)], g[1:2, :])
    m_ref[...] = jnp.full_like(m_ref, LOW)
    clear(l_ref, acc_ref)
    emit(
        forward_units(allowed(sc, partner, near), kne, ve, qn, m_ref, l_ref, acc_ref)
        + forward_units(allowed(sc, partner, far), knf, vf, qn, m_ref, l_ref, acc_ref)
    )
    for j in range(HB):
        total = l_ref[j]
        share = jnp.where(total > 0.0, 1.0 / jnp.where(total > 0.0, total, 1.0), 0.0)
        out = acc_ref[cols(j), :] * share
        o_ref[cols(j), :] = out.astype(BF)
        d_ref[j] = delta_row(out, do[:, cols(j)])
    for index, rows in enumerate((m_ref, l_ref, d_ref)):
        put_rows(ml_ref, index, rows)


def own_forward_far(
    sc, qn, knf, vf, do, acc0, ml0, mlp, acc_ref, st_ref, m_ref, l_ref, d_ref
):
    me, partner, near, far = around(sc)

    @pl.when(pl.program_id(0) == 0)
    def _():
        st_ref[mlp.shape[0] :, :] = mlp[...]

    get_rows(ml0, 0, m_ref)
    get_rows(ml0, 1, l_ref)
    acc_ref[...] = acc0[...]
    emit(forward_units(allowed(sc, me, far), knf, vf, qn, m_ref, l_ref, acc_ref))
    for j in range(HB):
        d_ref[j] = delta_row(acc_ref[cols(j), :] * (1.0 / l_ref[j]), do[:, cols(j)])
    for index, rows in enumerate((m_ref, l_ref, d_ref)):
        put_rows(st_ref, index, rows)


def weights_of(first, second, heads):
    m1, l1 = first[:heads], first[heads : 2 * heads]
    m2, l2 = second[:heads], second[heads : 2 * heads]
    m = jnp.maximum(m1, m2)
    w1, w2 = l1 * jnp.exp2(m1 - m), l2 * jnp.exp2(m2 - m)
    total = w1 + w2
    return w1 / total, w2 / total, m + jnp.log2(total)


def merge_stats(mine, got, o_ref, st_ref, sh_ref, o_out):
    o_out[...] = o_ref[...]

    @pl.when(pl.program_id(0) == 0)
    def _():
        size = mine.shape[0] // 2
        heads = size // 3
        both = ((mine[:size], got[size:]), (got[:size], mine[size:]))
        for half, (first, second) in enumerate(both):
            w1, w2, lse = weights_of(first, second, heads)
            base = 2 * half * heads
            st_ref[base : base + heads] = lse
            st_ref[base + heads : base + 2 * heads] = (
                w1 * first[2 * heads :] + w2 * second[2 * heads :]
            )
            if half == 0:
                total = first[heads : 2 * heads]
                sh_ref[:heads] = w1 / total
                sh_ref[heads:] = w2


def merge(acc_ref, sh, o_ret, _, att_ref):
    step = pl.program_id(0)
    heads = pl.num_programs(0) * HB
    for j in range(HB):
        c, h = cols(j), step * HB + j
        w1, w2 = sh[pl.ds(h, 1), :], sh[pl.ds(heads + h, 1), :]
        out = acc_ref[c, :] * w1 + o_ret[c, :].astype(F32) * w2
        att_ref[:, c] = jnp.transpose(out.astype(BF))


def stack(both, qn, do):
    @pl.when(pl.program_id(0) == 0)
    def _():
        both[:ROWS] = qn[...]
        both[ROWS:] = do[...]


def own_query_grads(
    sc, qn, do, st, knx, v, knp, vp, kne, ve, knf, vf, qs, ds, _, dq_ref, dk_ref, dv_ref, both_out
):
    me, partner, near, far = around(sc)
    stack(both_out, qs, ds)
    clear(dq_ref, dk_ref, dv_ref)

    def both(c, found):
        query_use(knx, dq_ref, c, found)
        key_use(qn, do, dk_ref, dv_ref, c, found)

    units = backward_units(None, knx, v, qn, do, st, both)
    for dev, kn, val in ((partner, knp, vp), (near, kne, ve), (far, knf, vf)):
        use = partial(query_use, kn, dq_ref)
        units += backward_units(allowed(sc, me, dev), kn, val, qn, do, st, use)
    emit(units)


def partner_query_grads(
    sc, qn, do, st, kne, ve, knf, vf, qs, ds, dq_ref, both_out, acc_ref
):
    me, partner, near, far = around(sc)
    stack(both_out, qs, ds)
    clear(acc_ref)
    units = []
    for dev, kn, val in ((near, kne, ve), (far, knf, vf)):
        use = partial(query_use, kn, acc_ref)
        units += backward_units(allowed(sc, partner, dev), kn, val, qn, do, st, use, 1)
    emit(units)
    dq_ref[...] = acc_ref[...].astype(BF)


def partner_near_grads(
    sc, knp, vp, qne, doe, ste, qs, ds, _, dk_ref, dv_ref, both_out, dk, dv
):
    me, partner, near, far = around(sc)
    stack(both_out, qs, ds)
    clear(dk, dv)
    back = partial(key_use, qne, doe, dk, dv)
    emit(backward_units(allowed(sc, near, partner), knp, vp, qne, doe, ste, back))
    dk_ref[...] = dk[...].astype(BF)
    dv_ref[...] = dv[...].astype(BF)


def partner_far_grads(chunk, heads, sc, knp, vp, both, st, dk0, dv0, _, out, dk, dv):
    me, partner, near, far = around(sc)
    dk[...] = dk0[...].astype(F32)
    dv[...] = dv0[...].astype(F32)
    qn, do = both.at[pl.ds(0, ROWS)], both.at[pl.ds(ROWS, ROWS)]
    use = partial(key_use, qn, do, dk, dv)
    emit(
        backward_units(
            allowed(sc, far, partner), knp, vp, qn, do, st, use, 1, chunk * HB, heads
        )
    )
    out[:ROWS] = dk[...].astype(BF)
    out[ROWS:] = dv[...].astype(BF)


def own_key_grads(sc, knx, v, qnp, dop, st, qne, doe, ste, dk0, dv0, *refs):
    dk, dv = refs[-2:]
    chunks = refs[:-3]
    me, partner, near, far = around(sc)
    dk[...] = dk0[...]
    dv[...] = dv0[...]
    own = partial(key_use, qnp, dop, dk, dv)
    use = partial(key_use, qne, doe, dk, dv)
    emit(
        backward_units(allowed(sc, partner, me), knx, v, qnp, dop, st, own, 1)
        + backward_units(allowed(sc, near, me), knx, v, qne, doe, ste, use)
    )
    for chunk, both in enumerate(chunks):
        @pl.when(pl.program_id(0) == chunk)
        def _(both=both):
            qn, do = both.at[pl.ds(0, ROWS)], both.at[pl.ds(ROWS, ROWS)]
            last = partial(key_use, qn, do, dk, dv)
            emit(backward_units(allowed(sc, far, me), knx, v, qn, do, ste, last, 1))


def finish_queries(g, dqt, dqr, q, _, dq_out):
    scale = 1.0 / math.sqrt(HD)
    for j in range(HB):
        c = cols(j)
        dq = jnp.transpose(dqt[c, :] + dqr[c, :].astype(F32)) * scale
        dq_out[:, c] = denormed(q[:, c], g[0:1, :], dq)


def finish_keys(g, k, dk, dv, *refs):
    dk_out, dv_out = refs[-2:]
    scale = 1.0 / math.sqrt(HD)
    for chunk, back in enumerate(refs[:-2]):
        @pl.when(pl.program_id(0) == chunk)
        def _(back=back):
            for j in range(HB):
                c = cols(j)
                total = (dk[:, c] + back[:ROWS, c].astype(F32)) * scale
                dk_out[:, c] = denormed(k[:, c], g[1:2, :], total)
            dv_out[...] = (dv[...] + back[ROWS:].astype(F32)).astype(BF)


WIDE = "wide"
TALL = "tall"
FULL = "full"
ORDER = "order"


def spec(kind, arr):
    if kind == WIDE:
        return pl.BlockSpec((ROWS, HB * HD), lambda i, *_: (0, i))
    if kind == TALL:
        return pl.BlockSpec((HB * HD, ROWS), lambda i, *_: (i, 0))
    if isinstance(kind, int):
        return pl.BlockSpec((ROWS, HB * HD), lambda i, *_: (0, kind))
    if kind == ORDER:
        return pl.BlockSpec(memory_space=pl.ANY)
    return pl.BlockSpec(arr.shape, lambda i, *_: (0,) * len(arr.shape))


def run(body, scalars, ins, outs, scratch=(), steps=None, name=None):
    if steps is None:
        steps = next(a.shape[1] for kind, a in ins if kind == WIDE) // (HB * HD)
    shapes = [jax.ShapeDtypeStruct(s, d) for _, s, d in outs]
    grid_spec = pltpu.PrefetchScalarGridSpec(
        num_scalar_prefetch=len(scalars),
        grid=(steps,),
        in_specs=[spec(kind, a) for kind, a in ins],
        out_specs=[spec(o[0], s) for o, s in zip(outs, shapes)],
        scratch_shapes=list(scratch),
    )
    return pl.pallas_call(
        body,
        name=name or body.__name__,
        grid_spec=grid_spec,
        out_shape=shapes,
        cost_estimate=pl.CostEstimate(
            flops=COST.get(name or body.__name__, OTHER),
            transcendentals=0,
            bytes_accessed=COST.get(name or body.__name__, OTHER),
        ),
        compiler_params=pltpu.CompilerParams(
            dimension_semantics=("arbitrary",), vmem_limit_bytes=32 << 20
        ),
    )(*scalars, *[a for _, a in ins])


def local(q_raw, k_raw, values_in, d_out, gains, tile_device, neighbours):
    count = lax.axis_size("ctx")
    inner = [(d, d ^ 1) for d in range(count)]
    outer = []
    for d in range(1, count - 1, 2):
        outer += [(d, d + 1), (d + 1, d)]
    q, k, v, do = q_raw[0], k_raw[0], values_in[0], d_out[0]
    features = q.shape[1]
    heads = features // HD

    def across(*values):
        return [lax.ppermute(value, "ctx", inner) for value in values]

    def beyond(*values):
        return [lax.ppermute(value, "ctx", outer) for value in values]

    wide_bf = (WIDE, (ROWS, features), BF)
    wide_f = (WIDE, (ROWS, features), F32)
    tall_bf = (TALL, (features, ROWS), BF)
    tall_f = (TALL, (features, ROWS), F32)
    stats = (FULL, (2 * heads, ROWS), F32)
    row_s = pltpu.VMEM((HB, 1, ROWS), F32)
    acc_t = pltpu.VMEM((HB * HD, ROWS), F32)
    acc_w = pltpu.VMEM((ROWS, HB * HD), F32)

    def wide(*arrays):
        return [(WIDE, a) for a in arrays]

    kp, vp = across(k, v)
    ke, ve = beyond(k, v)
    g = lax.all_gather(gains, "fsdp", axis=1, tiled=True)
    place = jnp.stack([lax.axis_index("ctx"), jnp.int32(count)]).astype(jnp.int32)
    scalars = (jnp.concatenate([place, tile_device, neighbours.reshape(-1)]),)
    gain = [(FULL, g)]
    chunks = features // (HB * HD)
    pair = (FULL, (2 * ROWS, HB * HD), BF)

    qn, knx, do2 = run(prepare, (), gain + wide(q, k, do), [wide_bf] * 3)
    kf, vf = beyond(kp, vp)
    qnp, dop = across(qn, do2)

    acc, ml, knp, kne, qn3, do3 = run(
        own_forward, scalars, gain + wide(qn, knx, v, kp, vp, ke, ve, do),
        [tall_f, stats] + [wide_bf] * 4, (row_s, row_s),
    )
    qne, doe = beyond(qn3, do3)
    parts = (FULL, (3 * heads, ROWS), F32)
    op, mlp, knf = run(
        partner_forward, scalars, gain + wide(qnp, kne, ve, kf, vf, dop),
        [tall_bf, parts, wide_bf], (row_s, row_s, row_s, acc_t),
    )
    acc, mine = run(
        own_forward_far, scalars,
        wide(qn, knf, vf, do) + [(TALL, acc), (FULL, ml), (FULL, mlp)],
        [tall_f, (FULL, (6 * heads, ROWS), F32)], (row_s, row_s, row_s),
    )
    (got,) = across(mine)
    st, shares, op = run(
        merge_stats, (), [(FULL, mine), (FULL, got), (TALL, op)],
        [(FULL, (4 * heads, ROWS), F32), stats, tall_bf], (), chunks,
    )
    (ste,) = beyond(st)
    (o_ret,) = across(op)

    def send(i):
        return [(i, qnp), (i, dop)]

    dqp, sent0 = run(
        partner_query_grads, scalars,
        wide(qnp, dop) + [(FULL, st)] + wide(kne, ve, knf, vf) + send(0),
        [tall_bf, pair], (acc_t,),
    )
    (dqr,) = across(dqp)
    dqt, dk, dv, sent1 = run(
        own_query_grads, scalars,
        wide(qn, do) + [(FULL, st)] + wide(knx, v, knp, vp, kne, ve, knf, vf) + send(1)
        + [(ORDER, dqp)],
        [tall_f, wide_f, wide_f, pair],
    )
    dkp, dvp, sent2 = run(
        partner_near_grads, scalars,
        wide(knp, vp, qne, doe) + [(FULL, ste)] + send(2) + [(ORDER, dqt)],
        [wide_bf, wide_bf, pair], (acc_w, acc_w),
    )
    far = beyond(sent0, sent1, sent2)
    (att,) = run(
        merge, (), [(TALL, acc), (FULL, shares), (TALL, o_ret), (ORDER, dkp)], [wide_bf], (), chunks,
    )
    last, back = att, []
    for i in range(chunks):
        (last,) = run(
            partial(partner_far_grads, i, heads), scalars,
            [(i, knp), (i, vp), (FULL, far[i]), (FULL, ste), (i, dkp), (i, dvp), (ORDER, last)],
            [pair], (acc_w, acc_w), 1, "partner_far_grads",
        )
        back += across(last)
    dk, dv = run(
        own_key_grads, scalars,
        wide(knx, v, qnp, dop) + [(FULL, st)] + wide(qne, doe) + [(FULL, ste)]
        + wide(dk, dv) + [(FULL, part) for part in far] + [(ORDER, last)],
        [wide_f, wide_f],
    )
    (dq_out,) = run(
        finish_queries, (), gain + [(TALL, dqt), (TALL, dqr)] + wide(q) + [(ORDER, dk)],
        [wide_bf],
    )
    dk_out, dv_out = run(
        finish_keys, (), gain + wide(k, dk, dv) + [(FULL, part) for part in back], [wide_bf] * 2
    )
    return att[None], dq_out[None], dk_out[None], dv_out[None]


def solution(mesh):
    tokens = P("fsdp", "ctx", None)
    return jax.shard_map(
        local,
        mesh=mesh,
        in_specs=(tokens, tokens, tokens, tokens, P(None, "fsdp"), P(), P()),
        out_specs=(tokens, tokens, tokens, tokens),
        check_vma=False,
    )
```

```python
import math
from functools import partial

import jax
import jax.numpy as jnp
from jax import lax
from jax.experimental import pallas as pl
from jax.experimental.pallas import tpu as pltpu
from jax.sharding import PartitionSpec as P

EPSILON = 1e-06
ROWS = 256
HD = 128
HB = 4
DEPTH = 1
LOW = -1e30
COST = dict.fromkeys(
    (
        "partner_forward",
        "own_forward_far",
        "merge_stats",
        "partner_query_grads",
        "own_query_grads",
    ),
    0,
) | {"partner_near_grads": 5_000_000_000}
CHUNKS = ((0, 2), (4, 4), (8, 4), (2, 2))
OTHER = 20_000_000_000
SCALE = math.log2(math.e) / math.sqrt(128)
BF = jnp.bfloat16
F32 = jnp.float32

NT = (((1,), (1,)), ((), ()))
TN = (((0,), (0,)), ((), ()))
NN = (((1,), (0,)), ((), ()))


def dot(a, b, dims):
    return lax.dot_general(a, b, dims, preferred_element_type=F32)


def allowed(sc, query_dev, key_dev):
    count = sc[1]
    inside = jnp.logical_and(
        jnp.logical_and(query_dev >= 0, query_dev < count),
        jnp.logical_and(key_dev >= 0, key_dev < count),
    )

    def tile_at(dev):
        first = 2 * (jnp.clip(dev, 0, count - 1) // 2)
        return jnp.where(sc[2 + first] == dev, first, first + 1)

    query_tile, key_tile = tile_at(query_dev), tile_at(key_dev)
    base = 2 + count + query_tile * 6
    hit = sc[base] == key_tile
    for slot in range(1, 6):
        hit = jnp.logical_or(hit, sc[base + slot] == key_tile)
    return jnp.logical_and(inside, hit)


def around(sc):
    me = sc[0]
    odd = me % 2 == 1
    partner = jnp.where(odd, me - 1, me + 1)
    near = jnp.where(odd, me + 1, me - 1)
    far = jnp.where(odd, me + 2, me - 2)
    return me, partner, near, far


def normed(raw, gain_row):
    floats = raw.astype(F32)
    inverse = lax.rsqrt(jnp.mean(floats * floats, axis=1, keepdims=True) + EPSILON)
    return (floats * inverse * gain_row).astype(BF)


def denormed(raw, gain_row, upstream):
    floats = raw.astype(F32)
    inverse = lax.rsqrt(jnp.mean(floats * floats, axis=1, keepdims=True) + EPSILON)
    scaled = upstream * gain_row
    inner = jnp.mean(floats * scaled, axis=1, keepdims=True)
    return (inverse * scaled - floats * (inverse * inverse * inverse * inner)).astype(BF)


def cols(j):
    return slice(j * HD, (j + 1) * HD)


def emit(units):
    first, second = {}, {}
    for t in range(len(units) + DEPTH + 1):
        if t < len(units):
            first[t] = units[t][0]()
        u = t - DEPTH - 1
        if u >= 0:
            units[u][2](second.pop(u))
        u = t - DEPTH
        if 0 <= u < len(units):
            second[u] = units[u][1](first.pop(u))


def forward_units(permit, kn, v, qn, m_ref, l_ref, acc_ref):
    units = []
    for j in range(HB):
        def scores(c=cols(j)):
            return dot(kn[:, c], qn[:, c], NT)

        def weights(s, j=j):
            top = jnp.max(s, axis=0, keepdims=True) * SCALE
            if permit is not None:
                top = jnp.where(permit, top, LOW)
            new = jnp.maximum(m_ref[j], top)
            shrink = jnp.exp2(m_ref[j] - new)
            m_ref[j] = new
            if permit is not None:
                new = jnp.where(permit, new, -LOW)
            return shrink, jnp.exp2(s * SCALE - new).astype(BF)

        def mix(found, j=j, c=cols(j)):
            shrink, p = found
            both = jnp.concatenate([v[:, c], jnp.ones((ROWS, HD), BF)], axis=1)
            out = dot(both, p, TN)
            l_ref[j] = l_ref[j] * shrink + out[HD : HD + 1]
            acc_ref[c, :] = acc_ref[c, :] * shrink + out[:HD]

        units.append((scores, weights, mix))
    return units


def backward_units(permit, kn, v, qn, do, st, use, half=0, first=None, heads=None, n=HB):
    if heads is None:
        heads = pl.num_programs(0) * HB
    if first is None:
        first = pl.program_id(0) * HB
    base = 2 * half * heads
    units = []
    for j in range(n):
        def scores(c=cols(j)):
            return dot(kn[:, c], qn[:, c], NT), dot(v[:, c], do[:, c], NT)

        def weights(found, h=base + first + j):
            s, dp = found
            lse = st[pl.ds(h, 1), :]
            if permit is not None:
                lse = jnp.where(permit, lse, -LOW)
            p = jnp.exp2(s * SCALE - lse)
            return p.astype(BF), (p * (dp - st[pl.ds(heads + h, 1), :])).astype(BF)

        units.append((scores, weights, partial(use, cols(j))))
    return units


def query_use(kn, dq_ref, c, found):
    dq_ref[c, :] += dot(kn[:, c], found[1], TN)


def key_use(qn, do, dk_ref, dv_ref, c, found):
    dk_ref[:, c] += dot(found[1], qn[:, c], NN)
    dv_ref[:, c] += dot(found[0], do[:, c], NN)


def clear(*refs):
    for ref in refs:
        ref[...] = jnp.zeros_like(ref)


def put_rows(ref, half, rows_ref):
    step = pl.program_id(0)
    heads = pl.num_programs(0) * HB
    for j in range(HB):
        ref[pl.ds(half * heads + step * HB + j, 1), :] = rows_ref[j]


def get_rows(ref, half, rows_ref):
    step = pl.program_id(0)
    heads = pl.num_programs(0) * HB
    for j in range(HB):
        rows_ref[j] = ref[pl.ds(half * heads + step * HB + j, 1), :]


def prepare(g, q, k, do, qn, kn, do_out):
    for j in range(HB):
        c = cols(j)
        qn[:, c] = normed(q[:, c], g[0:1, :])
        kn[:, c] = normed(k[:, c], g[1:2, :])
    do_out[...] = do[...]


def own_forward(
    sc, g, qn, knx, v, kp, vp, ke, ve, do, acc_ref, ml_ref, knp, kne, qn_out, do_out,
    m_ref, l_ref,
):
    me, partner, near, far = around(sc)
    qn_out[...] = qn[...]
    do_out[...] = do[...]
    for j in range(HB):
        c = cols(j)
        knp[:, c] = normed(kp[:, c], g[1:2, :])
        kne[:, c] = normed(ke[:, c], g[1:2, :])
    m_ref[...] = jnp.full_like(m_ref, LOW)
    clear(l_ref, acc_ref)
    emit(
        forward_units(None, knx, v, qn, m_ref, l_ref, acc_ref)
        + forward_units(allowed(sc, me, partner), knp, vp, qn, m_ref, l_ref, acc_ref)
        + forward_units(allowed(sc, me, near), kne, ve, qn, m_ref, l_ref, acc_ref)
    )
    put_rows(ml_ref, 0, m_ref)
    put_rows(ml_ref, 1, l_ref)


def delta_row(out, do):
    return jnp.sum(out * jnp.transpose(do).astype(F32), axis=0, keepdims=True)


def partner_forward(
    sc, g, qn, kne, ve, kf, vf, do, o_ref, ml_ref, knf, m_ref, l_ref, d_ref, acc_ref
):
    me, partner, near, far = around(sc)
    for j in range(HB):
        knf[:, cols(j)] = normed(kf[:, cols(j)], g[1:2, :])
    m_ref[...] = jnp.full_like(m_ref, LOW)
    clear(l_ref, acc_ref)
    emit(
        forward_units(allowed(sc, partner, near), kne, ve, qn, m_ref, l_ref, acc_ref)
        + forward_units(allowed(sc, partner, far), knf, vf, qn, m_ref, l_ref, acc_ref)
    )
    for j in range(HB):
        total = l_ref[j]
        share = jnp.where(total > 0.0, 1.0 / jnp.where(total > 0.0, total, 1.0), 0.0)
        out = acc_ref[cols(j), :] * share
        o_ref[cols(j), :] = out.astype(BF)
        d_ref[j] = delta_row(out, do[:, cols(j)])
    for index, rows in enumerate((m_ref, l_ref, d_ref)):
        put_rows(ml_ref, index, rows)


def own_forward_far(
    sc, qn, knf, vf, do, acc0, ml0, mlp, acc_ref, st_ref, m_ref, l_ref, d_ref
):
    me, partner, near, far = around(sc)

    @pl.when(pl.program_id(0) == 0)
    def _():
        st_ref[mlp.shape[0] :, :] = mlp[...]

    get_rows(ml0, 0, m_ref)
    get_rows(ml0, 1, l_ref)
    acc_ref[...] = acc0[...]
    emit(forward_units(allowed(sc, me, far), knf, vf, qn, m_ref, l_ref, acc_ref))
    for j in range(HB):
        d_ref[j] = delta_row(acc_ref[cols(j), :] * (1.0 / l_ref[j]), do[:, cols(j)])
    for index, rows in enumerate((m_ref, l_ref, d_ref)):
        put_rows(st_ref, index, rows)


def weights_of(first, second, heads):
    m1, l1 = first[:heads], first[heads : 2 * heads]
    m2, l2 = second[:heads], second[heads : 2 * heads]
    m = jnp.maximum(m1, m2)
    w1, w2 = l1 * jnp.exp2(m1 - m), l2 * jnp.exp2(m2 - m)
    total = w1 + w2
    return w1 / total, w2 / total, m + jnp.log2(total)


def merge_stats(mine, got, o_ref, st_ref, sh_ref, o_out):
    o_out[...] = o_ref[...]

    @pl.when(pl.program_id(0) == 0)
    def _():
        size = mine.shape[0] // 2
        heads = size // 3
        both = ((mine[:size], got[size:]), (got[:size], mine[size:]))
        for half, (first, second) in enumerate(both):
            w1, w2, lse = weights_of(first, second, heads)
            base = 2 * half * heads
            st_ref[base : base + heads] = lse
            st_ref[base + heads : base + 2 * heads] = (
                w1 * first[2 * heads :] + w2 * second[2 * heads :]
            )
            if half == 0:
                total = first[heads : 2 * heads]
                sh_ref[:heads] = w1 / total
                sh_ref[heads:] = w2


def merge(acc_ref, sh, o_ret, qs, ds, _, att_ref, both_out):
    stack(both_out, qs, ds)
    step = pl.program_id(0)
    heads = pl.num_programs(0) * HB
    for j in range(HB):
        c, h = cols(j), step * HB + j
        w1, w2 = sh[pl.ds(h, 1), :], sh[pl.ds(heads + h, 1), :]
        out = acc_ref[c, :] * w1 + o_ret[c, :].astype(F32) * w2
        att_ref[:, c] = jnp.transpose(out.astype(BF))


def stack(both, qn, do):
    @pl.when(pl.program_id(0) == 0)
    def _():
        both[:ROWS] = qn[...]
        both[ROWS:] = do[...]


def own_query_grads(
    sc, qn, do, st, knx, v, knp, vp, kne, ve, knf, vf, qs, ds, _, dq_ref, dk_ref, dv_ref, both_out
):
    me, partner, near, far = around(sc)
    stack(both_out, qs, ds)
    clear(dq_ref, dk_ref, dv_ref)

    def both(c, found):
        query_use(knx, dq_ref, c, found)
        key_use(qn, do, dk_ref, dv_ref, c, found)

    units = backward_units(None, knx, v, qn, do, st, both)
    for dev, kn, val in ((partner, knp, vp), (near, kne, ve), (far, knf, vf)):
        use = partial(query_use, kn, dq_ref)
        units += backward_units(allowed(sc, me, dev), kn, val, qn, do, st, use)
    emit(units)


def partner_query_grads(
    sc, qn, do, st, kne, ve, knf, vf, qs, ds, dq_ref, both_out, acc_ref
):
    me, partner, near, far = around(sc)
    stack(both_out, qs, ds)
    clear(acc_ref)
    units = []
    for dev, kn, val in ((near, kne, ve), (far, knf, vf)):
        use = partial(query_use, kn, acc_ref)
        units += backward_units(allowed(sc, partner, dev), kn, val, qn, do, st, use, 1)
    emit(units)
    dq_ref[...] = acc_ref[...].astype(BF)


def partner_near_grads(
    sc, knp, vp, qne, doe, ste, qs, ds, _, dk_ref, dv_ref, both_out, dk, dv
):
    me, partner, near, far = around(sc)
    stack(both_out, qs, ds)
    clear(dk, dv)
    back = partial(key_use, qne, doe, dk, dv)
    emit(backward_units(allowed(sc, near, partner), knp, vp, qne, doe, ste, back))
    dk_ref[...] = dk[...].astype(BF)
    dv_ref[...] = dv[...].astype(BF)


def partner_far_grads(start, n, heads, sc, knp, vp, both, st, dk0, dv0, _, __, out, dk, dv):
    me, partner, near, far = around(sc)
    dk[...] = dk0[...].astype(F32)
    dv[...] = dv0[...].astype(F32)
    qn, do = both.at[pl.ds(0, ROWS)], both.at[pl.ds(ROWS, ROWS)]
    use = partial(key_use, qn, do, dk, dv)
    emit(
        backward_units(
            allowed(sc, far, partner), knp, vp, qn, do, st, use, 1, start, heads, n
        )
    )
    out[:ROWS] = dk[...].astype(BF)
    out[ROWS:] = dv[...].astype(BF)


def own_key_grads(sc, knx, v, qnp, dop, st, qne, doe, ste, dk0, dv0, *refs):
    dk, dv = refs[-2:]
    chunks = refs[:-3]
    me, partner, near, far = around(sc)
    dk[...] = dk0[...]
    dv[...] = dv0[...]
    own = partial(key_use, qnp, dop, dk, dv)
    use = partial(key_use, qne, doe, dk, dv)
    emit(
        backward_units(allowed(sc, partner, me), knx, v, qnp, dop, st, own, 1)
        + backward_units(allowed(sc, near, me), knx, v, qne, doe, ste, use)
    )
    for (start, n), both in zip(CHUNKS, chunks):
        @pl.when(pl.program_id(0) == start // HB)
        def _(start=start, n=n, both=both):
            part = pl.ds(start % HB * HD, n * HD)
            qn, do = both.at[pl.ds(0, ROWS)], both.at[pl.ds(ROWS, ROWS)]
            last = partial(key_use, qn, do, dk.at[:, part], dv.at[:, part])
            heads = pl.num_programs(0) * HB
            emit(
                backward_units(
                    allowed(sc, far, me), knx.at[:, part], v.at[:, part], qn, do, ste, last,
                    1, start, heads, n,
                )
            )


def finish_queries(g, dqt, dqr, q, _, dq_out):
    scale = 1.0 / math.sqrt(HD)
    for j in range(HB):
        c = cols(j)
        dq = jnp.transpose(dqt[c, :] + dqr[c, :].astype(F32)) * scale
        dq_out[:, c] = denormed(q[:, c], g[0:1, :], dq)


def finish_keys(g, k, dk, dv, *refs):
    dk_out, dv_out = refs[-2:]
    scale = 1.0 / math.sqrt(HD)
    for (start, n), back in zip(CHUNKS, refs[:-2]):
        @pl.when(pl.program_id(0) == start // HB)
        def _(start=start, n=n, back=back):
            for j in range(n):
                c, b = cols(start % HB + j), cols(j)
                total = (dk[:, c] + back[:ROWS, b].astype(F32)) * scale
                dk_out[:, c] = denormed(k[:, c], g[1:2, :], total)
                dv_out[:, c] = (dv[:, c] + back[ROWS:, b].astype(F32)).astype(BF)


WIDE = "wide"
TALL = "tall"
FULL = "full"
ORDER = "order"


def spec(kind, arr):
    if kind == WIDE:
        return pl.BlockSpec((ROWS, HB * HD), lambda i, *_: (0, i))
    if kind == TALL:
        return pl.BlockSpec((HB * HD, ROWS), lambda i, *_: (i, 0))
    if isinstance(kind, tuple):
        start, n = kind
        return pl.BlockSpec((ROWS, n * HD), lambda i, *_: (0, start // n))
    if kind == ORDER:
        return pl.BlockSpec(memory_space=pl.ANY)
    return pl.BlockSpec(arr.shape, lambda i, *_: (0,) * len(arr.shape))


def run(body, scalars, ins, outs, scratch=(), steps=None, name=None):
    if steps is None:
        steps = next(a.shape[1] for kind, a in ins if kind == WIDE) // (HB * HD)
    shapes = [jax.ShapeDtypeStruct(s, d) for _, s, d in outs]
    grid_spec = pltpu.PrefetchScalarGridSpec(
        num_scalar_prefetch=len(scalars),
        grid=(steps,),
        in_specs=[spec(kind, a) for kind, a in ins],
        out_specs=[spec(o[0], s) for o, s in zip(outs, shapes)],
        scratch_shapes=list(scratch),
    )
    return pl.pallas_call(
        body,
        name=name or body.__name__,
        grid_spec=grid_spec,
        out_shape=shapes,
        cost_estimate=pl.CostEstimate(
            flops=COST.get(name or body.__name__, OTHER),
            transcendentals=0,
            bytes_accessed=COST.get(name or body.__name__, OTHER),
        ),
        compiler_params=pltpu.CompilerParams(
            dimension_semantics=("arbitrary",), vmem_limit_bytes=32 << 20
        ),
    )(*scalars, *[a for _, a in ins])


def local(q_raw, k_raw, values_in, d_out, gains, tile_device, neighbours):
    count = lax.axis_size("ctx")
    inner = [(d, d ^ 1) for d in range(count)]
    outer = []
    for d in range(1, count - 1, 2):
        outer += [(d, d + 1), (d + 1, d)]
    q, k, v, do = q_raw[0], k_raw[0], values_in[0], d_out[0]
    features = q.shape[1]
    heads = features // HD

    def across(*values):
        return [lax.ppermute(value, "ctx", inner) for value in values]

    def beyond(*values):
        return [lax.ppermute(value, "ctx", outer) for value in values]

    wide_bf = (WIDE, (ROWS, features), BF)
    wide_f = (WIDE, (ROWS, features), F32)
    tall_bf = (TALL, (features, ROWS), BF)
    tall_f = (TALL, (features, ROWS), F32)
    stats = (FULL, (2 * heads, ROWS), F32)
    row_s = pltpu.VMEM((HB, 1, ROWS), F32)
    acc_t = pltpu.VMEM((HB * HD, ROWS), F32)
    acc_w = pltpu.VMEM((ROWS, HB * HD), F32)

    def wide(*arrays):
        return [(WIDE, a) for a in arrays]

    kp, vp = across(k, v)
    ke, ve = beyond(k, v)
    g = lax.all_gather(gains, "fsdp", axis=1, tiled=True)
    place = jnp.stack([lax.axis_index("ctx"), jnp.int32(count)]).astype(jnp.int32)
    scalars = (jnp.concatenate([place, tile_device, neighbours.reshape(-1)]),)
    gain = [(FULL, g)]
    chunks = features // (HB * HD)
    pairs = [(FULL, (2 * ROWS, n * HD), BF) for _, n in CHUNKS]

    qn, knx, do2 = run(prepare, (), gain + wide(q, k, do), [wide_bf] * 3)
    kf, vf = beyond(kp, vp)
    qnp, dop = across(qn, do2)

    acc, ml, knp, kne, qn3, do3 = run(
        own_forward, scalars, gain + wide(qn, knx, v, kp, vp, ke, ve, do),
        [tall_f, stats] + [wide_bf] * 4, (row_s, row_s),
    )
    qne, doe = beyond(qn3, do3)
    parts = (FULL, (3 * heads, ROWS), F32)
    op, mlp, knf = run(
        partner_forward, scalars, gain + wide(qnp, kne, ve, kf, vf, dop),
        [tall_bf, parts, wide_bf], (row_s, row_s, row_s, acc_t),
    )
    acc, mine = run(
        own_forward_far, scalars,
        wide(qn, knf, vf, do) + [(TALL, acc), (FULL, ml), (FULL, mlp)],
        [tall_f, (FULL, (6 * heads, ROWS), F32)], (row_s, row_s, row_s),
    )
    (got,) = across(mine)
    st, shares, op = run(
        merge_stats, (), [(FULL, mine), (FULL, got), (TALL, op)],
        [(FULL, (4 * heads, ROWS), F32), stats, tall_bf], (), chunks,
    )
    (ste,) = beyond(st)
    (o_ret,) = across(op)

    def send(i):
        return [(CHUNKS[i], qnp), (CHUNKS[i], dop)]

    dqp, sent0 = run(
        partner_query_grads, scalars,
        wide(qnp, dop) + [(FULL, st)] + wide(kne, ve, knf, vf) + send(0),
        [tall_bf, pairs[0]], (acc_t,),
    )
    (dqr,) = across(dqp)
    dqt, dk, dv, sent1 = run(
        own_query_grads, scalars,
        wide(qn, do) + [(FULL, st)] + wide(knx, v, knp, vp, kne, ve, knf, vf) + send(1)
        + [(ORDER, dqp)],
        [tall_f, wide_f, wide_f, pairs[1]],
    )
    dkp, dvp, sent2 = run(
        partner_near_grads, scalars,
        wide(knp, vp, qne, doe) + [(FULL, ste)] + send(2) + [(ORDER, dqt)],
        [wide_bf, wide_bf, pairs[2]], (acc_w, acc_w),
    )
    far = beyond(sent0, sent1, sent2)
    last, back = dkp, []
    for i, (start, n) in enumerate(CHUNKS):
        at = (start, n)
        wait = o_ret if i == 0 else last
        acc_n = pltpu.VMEM((ROWS, n * HD), F32)
        (last,) = run(
            partial(partner_far_grads, start, n, heads), scalars,
            [(at, knp), (at, vp), (FULL, far[i]), (FULL, ste), (at, dkp), (at, dvp), (ORDER, last), (ORDER, wait)],
            [pairs[i]], (acc_n, acc_n), 1, "partner_far_grads",
        )
        back += across(last)
        if i == 0:
            att, sent3 = run(
                merge, (), [(TALL, acc), (FULL, shares), (TALL, o_ret)] + send(3) + [(ORDER, last)],
                [wide_bf, pairs[3]], (), chunks,
            )
            far += beyond(sent3)
            last = att
        if i == 1:
            (dq_out,) = run(
                finish_queries, (),
                gain + [(TALL, dqt), (TALL, dqr)] + wide(q) + [(ORDER, last)], [wide_bf],
            )
            last = dq_out
    dk, dv = run(
        own_key_grads, scalars,
        wide(knx, v, qnp, dop) + [(FULL, st)] + wide(qne, doe) + [(FULL, ste)]
        + wide(dk, dv) + [(FULL, part) for part in far] + [(ORDER, last)],
        [wide_f, wide_f],
    )
    dk_out, dv_out = run(
        finish_keys, (), gain + wide(k, dk, dv) + [(FULL, part) for part in back], [wide_bf] * 2
    )
    return att[None], dq_out[None], dk_out[None], dv_out[None]


def solution(mesh):
    tokens = P("fsdp", "ctx", None)
    return jax.shard_map(
        local,
        mesh=mesh,
        in_specs=(tokens, tokens, tokens, tokens, P(None, "fsdp"), P(), P()),
        out_specs=(tokens, tokens, tokens, tokens),
        check_vma=False,
    )
```

```python
import math
from functools import partial

import jax
import jax.numpy as jnp
from jax import lax
from jax.experimental import pallas as pl
from jax.experimental.pallas import tpu as pltpu
from jax.sharding import PartitionSpec as P

EPSILON = 1e-06
ROWS = 256
HD = 128
HB = 4
DEPTH = 1
LOW = -1e30
COST = dict.fromkeys(
    (
        "partner_forward",
        "own_forward_far",
        "merge_stats",
        "partner_query_grads",
        "own_query_grads",
    ),
    0,
) | {"partner_near_grads": 5_000_000_000}
CHUNKS = ((0, 2), (4, 4), (8, 4), (2, 2))
OTHER = 20_000_000_000
SCALE = math.log2(math.e) / math.sqrt(128)
BF = jnp.bfloat16
F32 = jnp.float32

NT = (((1,), (1,)), ((), ()))
TN = (((0,), (0,)), ((), ()))
NN = (((1,), (0,)), ((), ()))


def dot(a, b, dims):
    return lax.dot_general(a, b, dims, preferred_element_type=F32)


def allowed(sc, query_dev, key_dev):
    count = sc[1]
    inside = jnp.logical_and(
        jnp.logical_and(query_dev >= 0, query_dev < count),
        jnp.logical_and(key_dev >= 0, key_dev < count),
    )

    def tile_at(dev):
        first = 2 * (jnp.clip(dev, 0, count - 1) // 2)
        return jnp.where(sc[2 + first] == dev, first, first + 1)

    query_tile, key_tile = tile_at(query_dev), tile_at(key_dev)
    base = 2 + count + query_tile * 6
    hit = sc[base] == key_tile
    for slot in range(1, 6):
        hit = jnp.logical_or(hit, sc[base + slot] == key_tile)
    return jnp.logical_and(inside, hit)


def around(sc):
    me = sc[0]
    odd = me % 2 == 1
    partner = jnp.where(odd, me - 1, me + 1)
    near = jnp.where(odd, me + 1, me - 1)
    far = jnp.where(odd, me + 2, me - 2)
    return me, partner, near, far


def normed(raw, gain_row):
    floats = raw.astype(F32)
    inverse = lax.rsqrt(jnp.mean(floats * floats, axis=1, keepdims=True) + EPSILON)
    return (floats * inverse * gain_row).astype(BF)


def denormed(raw, gain_row, upstream):
    floats = raw.astype(F32)
    inverse = lax.rsqrt(jnp.mean(floats * floats, axis=1, keepdims=True) + EPSILON)
    scaled = upstream * gain_row
    inner = jnp.mean(floats * scaled, axis=1, keepdims=True)
    return (inverse * scaled - floats * (inverse * inverse * inverse * inner)).astype(BF)


def cols(j):
    return slice(j * HD, (j + 1) * HD)


def emit(units):
    first, second = {}, {}
    for t in range(len(units) + DEPTH + 1):
        if t < len(units):
            first[t] = units[t][0]()
        u = t - DEPTH - 1
        if u >= 0:
            units[u][2](second.pop(u))
        u = t - DEPTH
        if 0 <= u < len(units):
            second[u] = units[u][1](first.pop(u))


def forward_units(permit, kn, v, qn, m_ref, l_ref, acc_ref):
    units = []
    for j in range(HB):
        def scores(c=cols(j)):
            return dot(kn[:, c], qn[:, c], NT)

        def weights(s, j=j):
            top = jnp.max(s, axis=0, keepdims=True) * SCALE
            if permit is not None:
                top = jnp.where(permit, top, LOW)
            new = jnp.maximum(m_ref[j], top)
            shrink = jnp.exp2(m_ref[j] - new)
            m_ref[j] = new
            if permit is not None:
                new = jnp.where(permit, new, -LOW)
            return shrink, jnp.exp2(s * SCALE - new).astype(BF)

        def mix(found, j=j, c=cols(j)):
            shrink, p = found
            both = jnp.concatenate([v[:, c], jnp.ones((ROWS, HD), BF)], axis=1)
            out = dot(both, p, TN)
            l_ref[j] = l_ref[j] * shrink + out[HD : HD + 1]
            acc_ref[c, :] = acc_ref[c, :] * shrink + out[:HD]

        units.append((scores, weights, mix))
    return units


def backward_units(permit, kn, v, qn, do, st, use, half=0, first=None, heads=None, n=HB):
    if heads is None:
        heads = pl.num_programs(0) * HB
    if first is None:
        first = pl.program_id(0) * HB
    base = 2 * half * heads
    units = []
    for j in range(n):
        def scores(c=cols(j)):
            return dot(kn[:, c], qn[:, c], NT), dot(v[:, c], do[:, c], NT)

        def weights(found, h=base + first + j):
            s, dp = found
            lse = st[pl.ds(h, 1), :]
            if permit is not None:
                lse = jnp.where(permit, lse, -LOW)
            p = jnp.exp2(s * SCALE - lse)
            return p.astype(BF), (p * (dp - st[pl.ds(heads + h, 1), :])).astype(BF)

        units.append((scores, weights, partial(use, cols(j))))
    return units


def query_use(kn, dq_ref, c, found):
    dq_ref[c, :] += dot(kn[:, c], found[1], TN)


def key_use(qn, do, dk_ref, dv_ref, c, found):
    dk_ref[:, c] += dot(found[1], qn[:, c], NN)
    dv_ref[:, c] += dot(found[0], do[:, c], NN)


def clear(*refs):
    for ref in refs:
        ref[...] = jnp.zeros_like(ref)


def put_rows(ref, half, rows_ref):
    step = pl.program_id(0)
    heads = pl.num_programs(0) * HB
    for j in range(HB):
        ref[pl.ds(half * heads + step * HB + j, 1), :] = rows_ref[j]


def get_rows(ref, half, rows_ref):
    step = pl.program_id(0)
    heads = pl.num_programs(0) * HB
    for j in range(HB):
        rows_ref[j] = ref[pl.ds(half * heads + step * HB + j, 1), :]


def prepare(g, q, k, do, qn, kn, do_out):
    for j in range(HB):
        c = cols(j)
        qn[:, c] = normed(q[:, c], g[0:1, :])
        kn[:, c] = normed(k[:, c], g[1:2, :])
    do_out[...] = do[...]


def own_forward(
    sc, g, qn, knx, v, kp, vp, ke, ve, do, acc_ref, ml_ref, knp, kne, qn_out, do_out,
    m_ref, l_ref,
):
    me, partner, near, far = around(sc)
    qn_out[...] = qn[...]
    do_out[...] = do[...]
    for j in range(HB):
        c = cols(j)
        knp[:, c] = normed(kp[:, c], g[1:2, :])
        kne[:, c] = normed(ke[:, c], g[1:2, :])
    m_ref[...] = jnp.full_like(m_ref, LOW)
    clear(l_ref, acc_ref)
    emit(
        forward_units(None, knx, v, qn, m_ref, l_ref, acc_ref)
        + forward_units(allowed(sc, me, partner), knp, vp, qn, m_ref, l_ref, acc_ref)
        + forward_units(allowed(sc, me, near), kne, ve, qn, m_ref, l_ref, acc_ref)
    )
    put_rows(ml_ref, 0, m_ref)
    put_rows(ml_ref, 1, l_ref)


def delta_row(out, do):
    return jnp.sum(out * jnp.transpose(do).astype(F32), axis=0, keepdims=True)


def partner_forward(
    sc, g, qn, kne, ve, kf, vf, do, o_ref, ml_ref, knf, m_ref, l_ref, d_ref, acc_ref
):
    me, partner, near, far = around(sc)
    for j in range(HB):
        knf[:, cols(j)] = normed(kf[:, cols(j)], g[1:2, :])
    m_ref[...] = jnp.full_like(m_ref, LOW)
    clear(l_ref, acc_ref)
    emit(
        forward_units(allowed(sc, partner, near), kne, ve, qn, m_ref, l_ref, acc_ref)
        + forward_units(allowed(sc, partner, far), knf, vf, qn, m_ref, l_ref, acc_ref)
    )
    for j in range(HB):
        total = l_ref[j]
        share = jnp.where(total > 0.0, 1.0 / jnp.where(total > 0.0, total, 1.0), 0.0)
        out = acc_ref[cols(j), :] * share
        o_ref[cols(j), :] = out.astype(BF)
        d_ref[j] = delta_row(out, do[:, cols(j)])
    for index, rows in enumerate((m_ref, l_ref, d_ref)):
        put_rows(ml_ref, index, rows)


def own_forward_far(
    sc, qn, knf, vf, do, acc0, ml0, mlp, acc_ref, st_ref, m_ref, l_ref, d_ref
):
    me, partner, near, far = around(sc)

    @pl.when(pl.program_id(0) == 0)
    def _():
        st_ref[mlp.shape[0] :, :] = mlp[...]

    get_rows(ml0, 0, m_ref)
    get_rows(ml0, 1, l_ref)
    acc_ref[...] = acc0[...]
    emit(forward_units(allowed(sc, me, far), knf, vf, qn, m_ref, l_ref, acc_ref))
    for j in range(HB):
        d_ref[j] = delta_row(acc_ref[cols(j), :] * (1.0 / l_ref[j]), do[:, cols(j)])
    for index, rows in enumerate((m_ref, l_ref, d_ref)):
        put_rows(st_ref, index, rows)


def weights_of(first, second, heads):
    m1, l1 = first[:heads], first[heads : 2 * heads]
    m2, l2 = second[:heads], second[heads : 2 * heads]
    m = jnp.maximum(m1, m2)
    w1, w2 = l1 * jnp.exp2(m1 - m), l2 * jnp.exp2(m2 - m)
    total = w1 + w2
    return w1 / total, w2 / total, m + jnp.log2(total)


def merge_stats(mine, got, o_ref, st_ref, sh_ref, o_out):
    o_out[...] = o_ref[...]

    @pl.when(pl.program_id(0) == 0)
    def _():
        size = mine.shape[0] // 2
        heads = size // 3
        both = ((mine[:size], got[size:]), (got[:size], mine[size:]))
        for half, (first, second) in enumerate(both):
            w1, w2, lse = weights_of(first, second, heads)
            base = 2 * half * heads
            st_ref[base : base + heads] = lse
            st_ref[base + heads : base + 2 * heads] = (
                w1 * first[2 * heads :] + w2 * second[2 * heads :]
            )
            if half == 0:
                total = first[heads : 2 * heads]
                sh_ref[:heads] = w1 / total
                sh_ref[heads:] = w2


def merge(acc_ref, sh, o_ret, _, att_ref, token):
    clear(token)
    step = pl.program_id(0)
    heads = pl.num_programs(0) * HB
    for j in range(HB):
        c, h = cols(j), step * HB + j
        w1, w2 = sh[pl.ds(h, 1), :], sh[pl.ds(heads + h, 1), :]
        out = acc_ref[c, :] * w1 + o_ret[c, :].astype(F32) * w2
        att_ref[:, c] = jnp.transpose(out.astype(BF))


def stack(both, qn, do):
    @pl.when(pl.program_id(0) == 0)
    def _():
        both[:ROWS] = qn[...]
        both[ROWS:] = do[...]


def own_query_grads(
    sc, qn, do, st, knx, v, knp, vp, kne, ve, knf, vf, qs, ds, _, dq_ref, dk_ref, dv_ref, both_out
):
    me, partner, near, far = around(sc)
    stack(both_out, qs, ds)
    clear(dq_ref, dk_ref, dv_ref)

    def both(c, found):
        query_use(knx, dq_ref, c, found)
        key_use(qn, do, dk_ref, dv_ref, c, found)

    units = backward_units(None, knx, v, qn, do, st, both)
    for dev, kn, val in ((partner, knp, vp), (near, kne, ve), (far, knf, vf)):
        use = partial(query_use, kn, dq_ref)
        units += backward_units(allowed(sc, me, dev), kn, val, qn, do, st, use)
    emit(units)


def partner_query_grads(
    sc, qn, do, st, kne, ve, knf, vf, qs, ds, dq_ref, both_out, acc_ref
):
    me, partner, near, far = around(sc)
    stack(both_out, qs, ds)
    clear(acc_ref)
    units = []
    for dev, kn, val in ((near, kne, ve), (far, knf, vf)):
        use = partial(query_use, kn, acc_ref)
        units += backward_units(allowed(sc, partner, dev), kn, val, qn, do, st, use, 1)
    emit(units)
    dq_ref[...] = acc_ref[...].astype(BF)


def partner_near_grads(
    sc, knp, vp, qne, doe, ste, qs, ds, _, dk_ref, dv_ref, both_out, dk, dv
):
    me, partner, near, far = around(sc)
    stack(both_out, qs, ds)
    clear(dk, dv)
    back = partial(key_use, qne, doe, dk, dv)
    emit(backward_units(allowed(sc, near, partner), knp, vp, qne, doe, ste, back))
    dk_ref[...] = dk[...].astype(BF)
    dv_ref[...] = dv[...].astype(BF)


def partner_far_grads(start, n, heads, sc, knp, vp, both, st, dk0, dv0, _, __, out, dk, dv):
    me, partner, near, far = around(sc)
    dk[...] = dk0[...].astype(F32)
    dv[...] = dv0[...].astype(F32)
    qn, do = both.at[pl.ds(0, ROWS)], both.at[pl.ds(ROWS, ROWS)]
    use = partial(key_use, qn, do, dk, dv)
    emit(
        backward_units(
            allowed(sc, far, partner), knp, vp, qn, do, st, use, 1, start, heads, n
        )
    )
    out[:ROWS] = dk[...].astype(BF)
    out[ROWS:] = dv[...].astype(BF)


def own_key_grads(sc, knx, v, qnp, dop, st, qne, doe, ste, dk0, dv0, *refs):
    dk, dv = refs[-2:]
    chunks = refs[:-3]
    me, partner, near, far = around(sc)
    dk[...] = dk0[...]
    dv[...] = dv0[...]
    own = partial(key_use, qnp, dop, dk, dv)
    use = partial(key_use, qne, doe, dk, dv)
    emit(
        backward_units(allowed(sc, partner, me), knx, v, qnp, dop, st, own, 1)
        + backward_units(allowed(sc, near, me), knx, v, qne, doe, ste, use)
    )
    for (start, n), both in zip(CHUNKS, chunks):
        @pl.when(pl.program_id(0) == start // HB)
        def _(start=start, n=n, both=both):
            part = pl.ds(start % HB * HD, n * HD)
            qn, do = both.at[pl.ds(0, ROWS)], both.at[pl.ds(ROWS, ROWS)]
            last = partial(key_use, qn, do, dk.at[:, part], dv.at[:, part])
            heads = pl.num_programs(0) * HB
            emit(
                backward_units(
                    allowed(sc, far, me), knx.at[:, part], v.at[:, part], qn, do, ste, last,
                    1, start, heads, n,
                )
            )


def finish_queries(g, dqt, dqr, q, qs, ds, _, dq_out, both_out):
    stack(both_out, qs, ds)
    scale = 1.0 / math.sqrt(HD)
    for j in range(HB):
        c = cols(j)
        dq = jnp.transpose(dqt[c, :] + dqr[c, :].astype(F32)) * scale
        dq_out[:, c] = denormed(q[:, c], g[0:1, :], dq)


def finish_keys(g, k, dk, dv, *refs):
    dk_out, dv_out = refs[-2:]
    scale = 1.0 / math.sqrt(HD)
    for (start, n), back in zip(CHUNKS, refs[:-2]):
        @pl.when(pl.program_id(0) == start // HB)
        def _(start=start, n=n, back=back):
            for j in range(n):
                c, b = cols(start % HB + j), cols(j)
                total = (dk[:, c] + back[:ROWS, b].astype(F32)) * scale
                dk_out[:, c] = denormed(k[:, c], g[1:2, :], total)
                dv_out[:, c] = (dv[:, c] + back[ROWS:, b].astype(F32)).astype(BF)


WIDE = "wide"
TALL = "tall"
FULL = "full"
ORDER = "order"


def spec(kind, arr):
    if kind == WIDE:
        return pl.BlockSpec((ROWS, HB * HD), lambda i, *_: (0, i))
    if kind == TALL:
        return pl.BlockSpec((HB * HD, ROWS), lambda i, *_: (i, 0))
    if isinstance(kind, tuple):
        start, n = kind
        return pl.BlockSpec((ROWS, n * HD), lambda i, *_: (0, start // n))
    if kind == ORDER:
        return pl.BlockSpec(memory_space=pl.ANY)
    return pl.BlockSpec(arr.shape, lambda i, *_: (0,) * len(arr.shape))


def run(body, scalars, ins, outs, scratch=(), steps=None, name=None):
    if steps is None:
        steps = next(a.shape[1] for kind, a in ins if kind == WIDE) // (HB * HD)
    shapes = [jax.ShapeDtypeStruct(s, d) for _, s, d in outs]
    grid_spec = pltpu.PrefetchScalarGridSpec(
        num_scalar_prefetch=len(scalars),
        grid=(steps,),
        in_specs=[spec(kind, a) for kind, a in ins],
        out_specs=[spec(o[0], s) for o, s in zip(outs, shapes)],
        scratch_shapes=list(scratch),
    )
    return pl.pallas_call(
        body,
        name=name or body.__name__,
        grid_spec=grid_spec,
        out_shape=shapes,
        cost_estimate=pl.CostEstimate(
            flops=COST.get(name or body.__name__, OTHER),
            transcendentals=0,
            bytes_accessed=COST.get(name or body.__name__, OTHER),
        ),
        compiler_params=pltpu.CompilerParams(
            dimension_semantics=("arbitrary",), vmem_limit_bytes=32 << 20
        ),
    )(*scalars, *[a for _, a in ins])


def local(q_raw, k_raw, values_in, d_out, gains, tile_device, neighbours):
    count = lax.axis_size("ctx")
    inner = [(d, d ^ 1) for d in range(count)]
    outer = []
    for d in range(1, count - 1, 2):
        outer += [(d, d + 1), (d + 1, d)]
    q, k, v, do = q_raw[0], k_raw[0], values_in[0], d_out[0]
    features = q.shape[1]
    heads = features // HD

    def across(*values):
        return [lax.ppermute(value, "ctx", inner) for value in values]

    def beyond(*values):
        return [lax.ppermute(value, "ctx", outer) for value in values]

    wide_bf = (WIDE, (ROWS, features), BF)
    wide_f = (WIDE, (ROWS, features), F32)
    tall_bf = (TALL, (features, ROWS), BF)
    tall_f = (TALL, (features, ROWS), F32)
    stats = (FULL, (2 * heads, ROWS), F32)
    row_s = pltpu.VMEM((HB, 1, ROWS), F32)
    acc_t = pltpu.VMEM((HB * HD, ROWS), F32)
    acc_w = pltpu.VMEM((ROWS, HB * HD), F32)

    def wide(*arrays):
        return [(WIDE, a) for a in arrays]

    kp, vp = across(k, v)
    ke, ve = beyond(k, v)
    g = lax.all_gather(gains, "fsdp", axis=1, tiled=True)
    place = jnp.stack([lax.axis_index("ctx"), jnp.int32(count)]).astype(jnp.int32)
    scalars = (jnp.concatenate([place, tile_device, neighbours.reshape(-1)]),)
    gain = [(FULL, g)]
    chunks = features // (HB * HD)
    pairs = [(FULL, (2 * ROWS, n * HD), BF) for _, n in CHUNKS]

    qn, knx, do2 = run(prepare, (), gain + wide(q, k, do), [wide_bf] * 3)
    kf, vf = beyond(kp, vp)
    qnp, dop = across(qn, do2)

    acc, ml, knp, kne, qn3, do3 = run(
        own_forward, scalars, gain + wide(qn, knx, v, kp, vp, ke, ve, do),
        [tall_f, stats] + [wide_bf] * 4, (row_s, row_s),
    )
    qne, doe = beyond(qn3, do3)
    parts = (FULL, (3 * heads, ROWS), F32)
    op, mlp, knf = run(
        partner_forward, scalars, gain + wide(qnp, kne, ve, kf, vf, dop),
        [tall_bf, parts, wide_bf], (row_s, row_s, row_s, acc_t),
    )
    acc, mine = run(
        own_forward_far, scalars,
        wide(qn, knf, vf, do) + [(TALL, acc), (FULL, ml), (FULL, mlp)],
        [tall_f, (FULL, (6 * heads, ROWS), F32)], (row_s, row_s, row_s),
    )
    (got,) = across(mine)
    st, shares, op = run(
        merge_stats, (), [(FULL, mine), (FULL, got), (TALL, op)],
        [(FULL, (4 * heads, ROWS), F32), stats, tall_bf], (), chunks,
    )
    (ste,) = beyond(st)
    (o_ret,) = across(op)

    def send(i):
        return [(CHUNKS[i], qnp), (CHUNKS[i], dop)]

    dqp, sent0 = run(
        partner_query_grads, scalars,
        wide(qnp, dop) + [(FULL, st)] + wide(kne, ve, knf, vf) + send(0),
        [tall_bf, pairs[0]], (acc_t,),
    )
    (dqr,) = across(dqp)
    dqt, dk, dv, sent1 = run(
        own_query_grads, scalars,
        wide(qn, do) + [(FULL, st)] + wide(knx, v, knp, vp, kne, ve, knf, vf) + send(1)
        + [(ORDER, dqp)],
        [tall_f, wide_f, wide_f, pairs[1]],
    )
    dkp, dvp, sent2 = run(
        partner_near_grads, scalars,
        wide(knp, vp, qne, doe) + [(FULL, ste)] + send(2) + [(ORDER, dqt)],
        [wide_bf, wide_bf, pairs[2]], (acc_w, acc_w),
    )
    far = beyond(sent0, sent1, sent2)
    last, back = dkp, []
    for i, (start, n) in enumerate(CHUNKS):
        at = (start, n)
        wait = o_ret if i == 0 else last
        acc_n = pltpu.VMEM((ROWS, n * HD), F32)
        (last,) = run(
            partial(partner_far_grads, start, n, heads), scalars,
            [(at, knp), (at, vp), (FULL, far[i]), (FULL, ste), (at, dkp), (at, dvp), (ORDER, last), (ORDER, wait)],
            [pairs[i]], (acc_n, acc_n), 1, "partner_far_grads",
        )
        back += across(last)
        if i == 0:
            att, last = run(
                merge, (), [(TALL, acc), (FULL, shares), (TALL, o_ret), (ORDER, last)],
                [wide_bf, (FULL, (8, HD), F32)], (), chunks,
            )
        if i == 1:
            dq_out, sent3 = run(
                finish_queries, (),
                gain + [(TALL, dqt), (TALL, dqr)] + wide(q) + send(3) + [(ORDER, last)],
                [wide_bf, pairs[3]],
            )
            far += beyond(sent3)
            last = sent3
    dk, dv = run(
        own_key_grads, scalars,
        wide(knx, v, qnp, dop) + [(FULL, st)] + wide(qne, doe) + [(FULL, ste)]
        + wide(dk, dv) + [(FULL, part) for part in far] + [(ORDER, last)],
        [wide_f, wide_f],
    )
    dk_out, dv_out = run(
        finish_keys, (), gain + wide(k, dk, dv) + [(FULL, part) for part in back], [wide_bf] * 2
    )
    return att[None], dq_out[None], dk_out[None], dv_out[None]


def solution(mesh):
    tokens = P("fsdp", "ctx", None)
    return jax.shard_map(
        local,
        mesh=mesh,
        in_specs=(tokens, tokens, tokens, tokens, P(None, "fsdp"), P(), P()),
        out_specs=(tokens, tokens, tokens, tokens),
        check_vma=False,
    )
```
